32 devices in a mesh: fields: 2 (over y), rows: 4 (over z), cols: 2 (over x), sub: 2 (over core).
Axes of the slice: x: 2, y: 2, z: 4, core: 2. Of those that a mesh axis runs over, the one named last changes fastest.
Arguments:
- convergence: bfloat16 [32, 32, 16, 512], P(('fields', 'rows'), 'cols'), parts along dimension 0, may hold values from -6 to 6
- block_level: int32 [32, 32], P(('fields', 'rows'), 'cols'), parts along dimension 0, may hold values from 0 to 1
- near_codes: int32 [32, 32, 8], P(('fields', 'rows'), 'cols', 'sub'), parts along dimension 0, may hold values from 0 to 24, as said below
- far_rows: int32 [32, 32, 4], P(('fields', 'rows'), 'cols', 'sub'), parts along dimension 0, may hold values from 0 to 15, as said below
- near_factor: bfloat16 [512, 4096], P(None, 'sub'), may hold values from -0.09375 to 0.09375
- far_factor: bfloat16 [512, 2048], P(None, 'sub'), may hold values from -0.125 to 0.125
Outputs:
- whitened: bfloat16 [32, 32, 16, 512], P(('fields', 'rows'), 'cols', 'sub'), parts along dimension 0
The draws below stay inside these ranges and needn't reach their ends.
There are 2 independent parts, one for each index of `fields`. The reference program is written for one: setup_inputs(seed, part) draws one part's arguments, and reference() takes and returns one part's arrays. A program takes and returns all parts, laid end to end along the dimension named above; an argument that names none is the same for every part. Nothing has to cross between parts.
Inputs may be any that keep to these rules, and one draw needn't show every extreme that they name: `near_codes`: the 8 codes of a block are different from one another and never 12 (the block itself). `far_rows`: an entry never names a block row held by the same index of rows as the block. Among the 128 entries that one index of rows, cols and sub holds (slots 0 to 1 or 2 to 3), each other index of rows is named at most 64 times through its block rows, and one is named exactly 64 times.
All inputs are finite; a program needn't handle non-finite values.
Results may differ from the reference program's by a relative error of at most 0.001.
Values may be sent and summed in bfloat16 or wider, within the bound.
A program may use at most 64 MiB of HBM per device.

```python
import jax
import jax.numpy as jnp
from jax import lax

PIX = 512
NEAR = 8
FAR = 4
SAMPLES = 16
TILE_ROWS = 4
TILE_COLS = 16
BROWS = 16
BCOLS = 32
CAP = 64
N_ROWS = 4
N_COLS = 2


def draw_near_codes(key, part):
    scores = jax.random.randint(key, (BROWS, BCOLS, 24), 0, 2 ** 20) * 32 + jnp.arange(24, dtype=jnp.int32)
    ranked = jnp.argsort(scores, axis=-1)[..., :NEAR]
    return (ranked + (ranked >= 12)).astype(jnp.int32)


def draw_far_rows(key, part):
    group_count = N_ROWS * N_COLS * 2
    per_group = 2 * TILE_ROWS * TILE_COLS
    group_keys = jax.random.split(key, group_count)

    def draw_group(group_key, group_index):
        own_row = group_index // (N_COLS * 2)
        key_hot, key_pool, key_mix, key_inner = jax.random.split(group_key, 4)
        hot_source = jax.random.randint(key_hot, (), 0, N_ROWS - 1)
        spare_pool = jnp.arange((N_ROWS - 2) * CAP, dtype=jnp.int32) // CAP
        spare_pool = spare_pool + (spare_pool >= hot_source)
        spare_pool = jax.random.permutation(key_pool, spare_pool)[:per_group - CAP]
        chosen = jnp.concatenate([jnp.zeros((CAP,), jnp.int32) + hot_source, spare_pool])
        chosen = jax.random.permutation(key_mix, chosen)
        device = chosen + (chosen >= own_row)
        row_within = jax.random.randint(key_inner, (per_group,), 0, TILE_ROWS)
        return (device * TILE_ROWS + row_within).astype(jnp.int32)
    drawn = jax.vmap(draw_group)(group_keys, jnp.arange(group_count, dtype=jnp.int32))
    drawn = drawn.reshape(N_ROWS, N_COLS, 2, TILE_ROWS, TILE_COLS, 2)
    drawn = jnp.transpose(drawn, (0, 3, 1, 4, 2, 5))
    return drawn.reshape(BROWS, BCOLS, FAR).astype(jnp.int32)


def plant(array, stream_key, smallest, high):
    longest = array.shape.index(max(array.shape))
    spots = []
    for shift in (0, 1):
        where = [jax.random.randint(jax.random.fold_in(stream_key, axis), (), 0, length) for axis, length in enumerate(array.shape)]
        where[longest] = (where[longest] + shift) % array.shape[longest]
        spots.append(tuple(where))
    return array.at[spots[0]].set(smallest).at[spots[1]].set(high)


def shard_levels(own_key, shape, cuts, smallest, high):
    level = 1.0
    for dim, shards_of in cuts:
        steps = jax.random.uniform(jax.random.fold_in(jax.random.fold_in(own_key, 6), dim), (shards_of,), jnp.float32, smallest / len(cuts), high / len(cuts))
        level = level * jnp.repeat(jnp.exp(steps), shape[dim] // shards_of).reshape((-1,) + (1,) * (len(shape) - 1 - dim))
    return level


def scatter_about(rng, shape, scale, reach, cuts=(), held_as=jnp.bfloat16):
    array = jax.random.normal(rng, shape, jnp.float32) * scale
    if len(cuts) > 0:
        array = shard_levels(rng, shape, cuts, -0.22, 0.18) * array
    return jnp.clip(array, min=-reach, max=reach).astype(held_as)


def setup_inputs(seed: int = 0, part: int = 0) -> dict:
    key_of = jax.random.split(jax.random.key(seed), 7)
    part_keys = jax.random.split(jax.random.fold_in(key_of[6], part), 7)
    convergence = scatter_about(part_keys[0], (BROWS, BCOLS, SAMPLES, PIX), 1.0, 6.0, ((0, 4), (1, 2)))
    block_level = plant(jax.random.randint(part_keys[1], (BROWS, BCOLS), 0, 2), jax.random.fold_in(part_keys[1], 1), 0, 1).astype(jnp.int32)
    near_codes = draw_near_codes(jax.random.fold_in(jax.random.fold_in(key_of[6], part), 71), part)
    far_rows = draw_far_rows(jax.random.fold_in(jax.random.fold_in(key_of[6], part), 71), part)
    near_factor = scatter_about(key_of[4], (PIX, NEAR * PIX), (NEAR * PIX) ** -0.5, 0.09375, ((1, 2),))
    far_factor = scatter_about(key_of[5], (PIX, FAR * PIX), (FAR * PIX) ** -0.5, 0.125, ((1, 2),))
    return {"convergence": convergence, "block_level": block_level, "near_codes": near_codes, "far_rows": far_rows, "near_factor": near_factor, "far_factor": far_factor}


def reference(convergence, block_level, near_codes, far_rows, near_factor, far_factor):
    padded = jnp.pad(convergence, ((2, 2), (2, 2), (0, 0), (0, 0)))
    near_weight = near_factor.astype(jnp.float32).reshape(PIX, NEAR, PIX)
    far_weight = far_factor.astype(jnp.float32).reshape(PIX, FAR, PIX)
    columns = jnp.arange(BCOLS, dtype=jnp.int32)

    def one_row(row):
        codes = near_codes[row]
        row_index = (row + codes // 5).astype(jnp.int32)
        col_index = (columns[:, None] + codes % 5).astype(jnp.int32)
        near_blocks = padded[row_index, col_index].astype(jnp.float32)
        near_term = jnp.einsum("cksq,pkq->csp", near_blocks, near_weight)
        far_blocks = convergence[far_rows[row].astype(jnp.int32), columns[:, None]].astype(jnp.float32)
        far_term = jnp.einsum("cksq,pkq->csp", far_blocks, far_weight)
        mean = jnp.where(block_level[row][:, None, None] == 1, near_term, far_term)
        return (convergence[row].astype(jnp.float32) - mean).astype(jnp.bfloat16)

    return lax.map(one_row, jnp.arange(BROWS, dtype=jnp.int32))
```

```python
import functools

import jax
import jax.numpy as jnp
from jax import lax
from jax.experimental import pallas as pl
from jax.experimental.pallas import tpu as pltpu
from jax.sharding import PartitionSpec as P

MESH = pl.DeviceIdType.MESH
PARTS = 4


def chunk_starts(cols):
    return [0, cols * 5 // 16, cols * 10 // 16, cols * 14 // 16, cols]


def kernel(dims, conv, codes, near_factor, far_factor, out, *scratch):
    n_rows, n_cols, tile_rows, tile_cols, half, pixels, near_slots, far_slots = dims
    starts = chunk_starts(tile_cols)
    chunks = len(starts) - 1
    sizes = [starts[k + 1] - starts[k] for k in range(chunks)]
    far = scratch[:chunks]
    (near, near_w, far_w, codes_v, codes_s, near_g, far_g, near_acc, far_acc, end_acc,
     white_src, white_dst, tile_send, tile_recv, white_send, white_recv,
     side_send, side_recv, corner_send, corner_recv, code_send, code_recv, fac_send, fac_recv, loc_sem, halo_sem) = scratch[chunks:]

    i = lax.axis_index("rows")
    x = lax.axis_index("cols")
    s = lax.axis_index("sub")
    other = 1 - s
    mine = pl.ds(pl.multiple_of(s * half, half), half)
    is_end = (i == 0) | (i == n_rows - 1)
    is_mid = (i > 0) & (i < n_rows - 1)
    low_helper = i == 1
    high_helper = i == n_rows - 2
    is_helper = low_helper | high_helper
    end_tile = jnp.where(low_helper, 0, n_rows - 1)
    to_mid = jnp.where(i == 0, 1, n_rows - 2)

    def cols_of(k):
        return pl.ds(starts[k], sizes[k])

    local = [
        pltpu.make_async_copy(
            conv.at[:, :, mine, :],
            near.at[pl.ds(2, tile_rows), pl.ds(2, tile_cols)],
            loc_sem.at[0],
        ),
        pltpu.make_async_copy(near_factor, near_w.at[s], loc_sem.at[1]),
        pltpu.make_async_copy(far_factor, far_w.at[s], loc_sem.at[2]),
        pltpu.make_async_copy(codes, codes_s.at[0, s], loc_sem.at[3]),
    ]
    for copy in local:
        copy.start()
    own_far = [
        pltpu.make_async_copy(
            conv.at[:, cols_of(k), mine, :],
            far[k].at[pl.ds(i * tile_rows, tile_rows)],
            loc_sem.at[6 + k],
        )
        for k in range(chunks)
    ]

    @pl.when(is_mid)
    def _():
        for copy in own_far:
            copy.start()

    @pl.when(i == 0)
    def _():
        near[0:2] = jnp.zeros((2,) + near.shape[1:], near.dtype)

    @pl.when(i == n_rows - 1)
    def _():
        near[tile_rows + 2:tile_rows + 4] = jnp.zeros((2,) + near.shape[1:], near.dtype)

    @pl.when(x == 0)
    def _():
        near[:, 0:2] = jnp.zeros((near.shape[0], 2) + near.shape[2:], near.dtype)

    @pl.when(x == n_cols - 1)
    def _():
        near[:, tile_cols + 2:tile_cols + 4] = jnp.zeros((near.shape[0], 2) + near.shape[2:], near.dtype)

    barrier = pltpu.get_barrier_semaphore()
    offsets = [(-1, 0), (1, 0), (0, -1), (0, 1)]

    def present(di, dx):
        ok = jnp.bool_(True)
        if di == -1:
            ok = ok & (i > 0)
        if di == 1:
            ok = ok & (i < n_rows - 1)
        if dx == -1:
            ok = ok & (x > 0)
        if dx == 1:
            ok = ok & (x < n_cols - 1)
        return ok

    for di, dx in offsets:
        @pl.when(present(di, dx))
        def _():
            pl.semaphore_signal(barrier, inc=1, device_id={"rows": i + di, "cols": x + dx}, device_id_type=MESH)
    pl.semaphore_signal(barrier, inc=1, device_id={"sub": other}, device_id_type=MESH)
    count_z = (i > 0).astype(jnp.int32) + (i < n_rows - 1).astype(jnp.int32)
    count_x = (x > 0).astype(jnp.int32) + (x < n_cols - 1).astype(jnp.int32)
    pl.semaphore_wait(barrier, count_z + count_x + 1)

    def code_copy(which, slot, target):
        return pltpu.make_async_remote_copy(
            src_ref=codes if which < 2 else codes_v.at[slot, s], dst_ref=codes_v.at[slot, s],
            send_sem=code_send.at[which], recv_sem=code_recv.at[which], device_id=target, device_id_type=MESH)

    code_partner = code_copy(0, 0, {"sub": other})
    code_straight = code_copy(1, 1, {"rows": to_mid})
    code_relay = code_copy(2, 1, {"sub": other})
    code_partner.start()

    @pl.when(is_end)
    def _():
        code_straight.start()

    def side_copy(di, dx):
        if di == 0:
            rows_src, rows_dst = pl.ds(0, tile_rows), pl.ds(2, tile_rows)
        elif di == -1:
            rows_src, rows_dst = pl.ds(0, 2), pl.ds(tile_rows + 2, 2)
        else:
            rows_src, rows_dst = pl.ds(tile_rows - 2, 2), pl.ds(0, 2)
        if dx == 0:
            cols_src, cols_dst = pl.ds(0, tile_cols), pl.ds(2, tile_cols)
        elif dx == -1:
            cols_src, cols_dst = pl.ds(0, 2), pl.ds(tile_cols + 2, 2)
        else:
            cols_src, cols_dst = pl.ds(tile_cols - 2, 2), pl.ds(0, 2)
        which = offsets.index((di, dx))
        return pltpu.make_async_remote_copy(
            src_ref=conv.at[rows_src, cols_src, mine, :],
            dst_ref=near.at[rows_dst, cols_dst],
            send_sem=side_send.at[which], recv_sem=side_recv.at[which],
            device_id={"rows": i + di, "cols": x + dx}, device_id_type=MESH)

    def side_sends(di, dx):
        if dx == 0:
            return low_helper if di == -1 else high_helper
        return present(di, dx)

    def side_receives(di, dx):
        if dx == 0:
            return (i == 0) if di == -1 else (i == n_rows - 1)
        return present(-di, -dx)

    def tile_copy(way, d, k, tile):
        src = conv.at[:, cols_of(k), mine, :] if d == 0 else far[k].at[pl.ds(tile * tile_rows, tile_rows)]
        return pltpu.make_async_remote_copy(
            src_ref=src, dst_ref=far[k].at[pl.ds(tile * tile_rows, tile_rows)],
            send_sem=tile_send.at[way, d, k], recv_sem=tile_recv.at[way, d, k],
            device_id={"rows": i - 1 if way == 0 else i + 1}, device_id_type=MESH)

    def sent(way, d, k):
        return tile_copy(way, d, k, i + d if way == 0 else i - d)

    def received(way, d, k):
        return tile_copy(way, d, k, i + 1 + d if way == 0 else i - 1 - d)

    def tile_sends(way, d):
        if way == 0:
            return (i >= 2) & (i + d <= n_rows - 1)
        return (i <= n_rows - 3) & (i - d >= 0)

    def tile_receives(way, d):
        if way == 0:
            return is_mid & (i + 1 + d <= n_rows - 1)
        return is_mid & (i - 1 - d >= 0)

    for k in range(chunks):
        for way in (0, 1):
            @pl.when(tile_sends(way, 0))
            def _():
                sent(way, 0, k).start()
        if k == 0:
            for di, dx in offsets:
                @pl.when(side_sends(di, dx))
                def _():
                    side_copy(di, dx).start()

    def factor_copy(which):
        src, dst = ((near_factor, near_w), (far_factor, far_w))[which]
        return pltpu.make_async_remote_copy(
            src_ref=src, dst_ref=dst.at[s], send_sem=fac_send.at[which],
            recv_sem=fac_recv.at[which], device_id={"sub": other}, device_id_type=MESH)

    for which in (0, 1):
        factor_copy(which).start()

    def halo_copy(way, k):
        if way == 0:
            src_rows, dst_rows = pl.ds((i + 1) * tile_rows, 2), pl.ds(tile_rows + 2, 2)
        else:
            src_rows, dst_rows = pl.ds(i * tile_rows - 2, 2), pl.ds(0, 2)
        return pltpu.make_async_copy(
            far[k].at[src_rows], near.at[dst_rows, pl.ds(2 + starts[k], sizes[k])], halo_sem.at[way, k])

    for d in range(n_rows - 3):
        for k in range(chunks):
            for way in (0, 1):
                @pl.when(tile_receives(way, d))
                def _():
                    received(way, d, k).wait_recv()
                    if d == 0:
                        halo_copy(way, k).start()

                @pl.when(tile_sends(way, d + 1))
                def _():
                    sent(way, d + 1, k).start()

    code_copy(0, 0, {"sub": other}).wait_recv()
    code_in = pltpu.make_async_copy(codes_v.at[0, other], codes_s.at[0, other], loc_sem.at[4])
    code_in.start()
    end_codes = pltpu.make_async_copy(codes_v.at[1], codes_s.at[1], loc_sem.at[5])

    @pl.when(is_helper)
    def _():
        code_straight.wait_recv()
        code_relay.start()

    for copy in local:
        copy.wait()

    @pl.when(is_mid)
    def _():
        for k in range(chunks):
            halo_copy(0, k).wait()
            halo_copy(1, k).wait()
            own_far[k].wait()

    for di, dx in offsets:
        @pl.when(side_receives(di, dx))
        def _():
            side_copy(di, dx).wait_recv()

    def corner_copy(di, dx):
        rows = pl.ds(0, 2) if di == -1 else pl.ds(tile_rows + 2, 2)
        src, dst = (2, tile_cols + 2) if dx == -1 else (tile_cols, 0)
        which = (di + 1) + (dx + 1) // 2
        return pltpu.make_async_remote_copy(
            src_ref=near.at[rows, pl.ds(src, 2)], dst_ref=near.at[rows, pl.ds(dst, 2)],
            send_sem=corner_send.at[which], recv_sem=corner_recv.at[which],
            device_id={"cols": x + dx}, device_id_type=MESH)

    corners = [(di, dx) for di in (-1, 1) for dx in (-1, 1)]
    for di, dx in corners:
        @pl.when(present(di, 0) & present(0, dx))
        def _():
            corner_copy(di, dx).start()

    @pl.when(is_helper)
    def _():
        code_relay.wait_recv()
        end_codes.start()
        end_codes.wait()

    code_in.wait()
    for which in (0, 1):
        factor_copy(which).wait_recv()
    for di, dx in corners:
        @pl.when(present(di, 0) & present(0, -dx))
        def _():
            corner_copy(di, dx).wait_recv()

    contract = (((1,), (1,)), ((), ()))
    part_slots = 2 * near_slots // PARTS

    def block_rows(block):
        return pl.ds(pl.multiple_of(block * half, half), half)

    def pair_rows(block):
        return pl.ds(pl.multiple_of(block * half, 2 * half), 2 * half)

    def joined(first, second):
        both = jnp.concatenate([first.astype(jnp.float32), second.astype(jnp.float32)], axis=0)
        return both.astype(jnp.bfloat16)

    def near_part(part):
        sub, base = part * part_slots // near_slots, part * part_slots % near_slots

        def near_block(r, c, slot):
            code = codes_s[0, sub, r, base + slot, c]
            down = lax.shift_right_logical(code * 205, 10)
            return near[r + down, c + code - 5 * down]

        def gather(c, carry):
            for r in range(0, tile_rows, 2):
                for slot in range(part_slots):
                    near_g[pair_rows(c * tile_rows + r), slot * pixels:(slot + 1) * pixels] = joined(
                        near_block(r, c, slot), near_block(r + 1, c, slot))
            return carry

        lax.fori_loop(0, tile_cols, gather, 0)
        product = lax.dot_general(
            near_g[...], near_w[sub, :, base * pixels:(base + part_slots) * pixels], contract,
            preferred_element_type=jnp.float32)
        if part == 0:
            near_acc[...] = product
        else:
            near_acc[...] += product

    level_at = near_slots + far_slots

    def far_chunk(k):
        rows = sizes[k] * tile_rows * half

        def gather_far(who):
            def far_block(r, c, sub, slot):
                row = codes_s[who, sub, r, near_slots + slot, starts[k] + c]
                return far[k][row, c]

            def body(c, carry):
                for r in range(0, tile_rows, 2):
                    for sub in range(2):
                        for slot in range(far_slots):
                            at = sub * far_slots + slot
                            far_g[pair_rows((who * sizes[k] + c) * tile_rows + r), at * pixels:(at + 1) * pixels] = joined(
                                far_block(r, c, sub, slot), far_block(r + 1, c, sub, slot))
                return carry

            lax.fori_loop(0, sizes[k], body, 0)

        gather_far(0)

        @pl.when(is_helper)
        def _():
            gather_far(1)

        depth = far_slots * pixels
        product = lax.dot_general(
            far_g[:2 * rows, :depth], far_w[0], contract, preferred_element_type=jnp.float32)
        product += lax.dot_general(
            far_g[:2 * rows, depth:], far_w[1], contract, preferred_element_type=jnp.float32)
        far_acc[pl.ds(starts[k] * tile_rows * half, rows), :] = product[:rows]
        end_acc[pl.ds(0, rows), :] = product[rows:]

        @pl.when(is_helper)
        def _():
            def body(c, carry):
                for r in range(tile_rows):
                    value = far[k][end_tile * tile_rows + r, c].astype(jnp.float32)
                    white_src[r, starts[k] + c] = (value - end_acc[block_rows(c * tile_rows + r), :]).astype(jnp.bfloat16)
                return carry

            lax.fori_loop(0, sizes[k], body, 0)
            white_copy(k).start()

    def white_copy(k):
        return pltpu.make_async_remote_copy(
            src_ref=white_src.at[:, cols_of(k)], dst_ref=white_dst.at[:, cols_of(k)],
            send_sem=white_send.at[k], recv_sem=white_recv.at[k],
            device_id={"rows": end_tile}, device_id_type=MESH)

    @pl.when(is_mid)
    def _():
        near_part(0)
        for k in range(chunks):
            d = n_rows - 3
            for way in (0, 1):
                @pl.when(tile_receives(way, d))
                def _():
                    received(way, d, k).wait_recv()
            far_chunk(k)
            if k < PARTS - 2:
                near_part(k + 1)
        near_part(PARTS - 1)

        def body(c, carry):
            for r in range(tile_rows):
                level = codes_s[0, s, r, level_at, c]
                at = block_rows(c * tile_rows + r)
                mean = jnp.where(level == 1, near_acc[at, :], far_acc[at, :])
                out[r, c] = (near[2 + r, 2 + c].astype(jnp.float32) - mean).astype(jnp.bfloat16)
            return carry

        lax.fori_loop(0, tile_cols, body, 0)

    @pl.when(is_end)
    def _():
        for part in range(PARTS):
            near_part(part)
        for k in range(chunks):
            white_copy(k).wait_recv()

            def body(c, carry):
                for r in range(tile_rows):
                    level = codes_s[0, s, r, level_at, c]
                    mean = near_acc[block_rows(c * tile_rows + r), :]
                    fine = near[2 + r, 2 + c].astype(jnp.float32) - mean
                    coarse = white_dst[r, c].astype(jnp.float32)
                    out[r, c] = jnp.where(level == 1, fine, coarse).astype(jnp.bfloat16)
                return carry

            lax.fori_loop(starts[k], starts[k + 1], body, 0)

    code_partner.wait_send()

    @pl.when(is_end)
    def _():
        code_straight.wait_send()

    for di, dx in corners:
        @pl.when(present(di, 0) & present(0, dx))
        def _():
            corner_copy(di, dx).wait_send()

    for di, dx in offsets:
        @pl.when(side_sends(di, dx))
        def _():
            side_copy(di, dx).wait_send()
    for which in (0, 1):
        factor_copy(which).wait_send()
    for d in range(n_rows - 2):
        for way in (0, 1):
            @pl.when(tile_sends(way, d))
            def _():
                for k in range(chunks):
                    sent(way, d, k).wait_send()

    @pl.when(is_helper)
    def _():
        code_relay.wait_send()
        for k in range(chunks):
            white_copy(k).wait_send()


def on_device(convergence, block_level, near_codes, far_rows, near_factor, far_factor):
    tile_rows, tile_cols, samples, pixels = convergence.shape
    n_rows, n_cols = lax.axis_size("rows"), lax.axis_size("cols")
    near_slots, far_slots = near_codes.shape[2], far_rows.shape[2]
    half = samples // 2
    starts = chunk_starts(tile_cols)
    chunks = len(starts) - 1
    codes = jnp.concatenate(
        [jnp.transpose(near_codes, (0, 2, 1)), jnp.transpose(far_rows, (0, 2, 1)), block_level[:, None, :]], axis=1)
    dims = (n_rows, n_cols, tile_rows, tile_cols, half, pixels, near_slots, far_slots)
    block = (half, pixels)
    bf16, f32 = jnp.bfloat16, jnp.float32
    all_rows = tile_rows * tile_cols * half
    chunk_rows = tile_rows * half * max(starts[k + 1] - starts[k] for k in range(chunks))
    dma = pltpu.SemaphoreType.DMA
    scratch = [pltpu.VMEM((n_rows * tile_rows, starts[k + 1] - starts[k]) + block, bf16) for k in range(chunks)]
    scratch += [
        pltpu.VMEM((tile_rows + 4, tile_cols + 4) + block, bf16),
        pltpu.VMEM((2,) + near_factor.shape, bf16),
        pltpu.VMEM((2,) + far_factor.shape, bf16),
        pltpu.VMEM((2, 2) + codes.shape, jnp.int32),
        pltpu.SMEM((2, 2) + codes.shape, jnp.int32),
        pltpu.VMEM((all_rows, 2 * near_slots // PARTS * pixels), bf16),
        pltpu.VMEM((2 * chunk_rows, 2 * far_slots * pixels), bf16),
        pltpu.VMEM((all_rows, pixels), f32),
        pltpu.VMEM((all_rows, pixels), f32),
        pltpu.VMEM((chunk_rows, pixels), f32),
        pltpu.VMEM((tile_rows, tile_cols) + block, bf16),
        pltpu.VMEM((tile_rows, tile_cols) + block, bf16),
        dma((2, n_rows - 2, chunks)),
        dma((2, n_rows - 2, chunks)),
        dma((chunks,)),
        dma((chunks,)),
        dma((4,)),
        dma((4,)),
        dma((4,)),
        dma((4,)),
        dma((3,)),
        dma((3,)),
        dma((2,)),
        dma((2,)),
        dma((6 + chunks,)),
        dma((2, chunks)),
    ]
    anywhere = pl.BlockSpec(memory_space=pl.ANY)
    vmem = pl.BlockSpec(memory_space=pltpu.VMEM)
    return pl.pallas_call(
        functools.partial(kernel, dims),
        out_shape=jax.ShapeDtypeStruct((tile_rows, tile_cols) + block, bf16),
        in_specs=[anywhere, vmem, anywhere, anywhere],
        out_specs=vmem,
        scratch_shapes=scratch,
        compiler_params=pltpu.CompilerParams(
            collective_id=0, has_side_effects=True, vmem_limit_bytes=56 * 1024 * 1024),
    )(convergence, codes, near_factor, far_factor)


def group_starts(cols, served):
    left = cols - 2 * served
    return [2 * served, 2 * served + left // 2, 2 * served + left * 3 // 4, cols]


def pair_kernel(dims, conv, near_codes, far_codes, levels, near_factor, far_factor, out, *scratch):
    n_rows, n_cols, tile_rows, tile_cols, half, pixels, near_slots, far_slots, served = dims
    starts = group_starts(tile_cols, served)
    chunks = len(starts) - 1
    sizes = [starts[k + 1] - starts[k] for k in range(chunks)]
    far_both = scratch[:chunks]
    (far_served, near, stage, near_w, far_w, near_codes_v, far_codes_v, near_codes_s, far_codes_s, levels_s,
     near_g, far_g, near_acc, far_acc, white_served, white_both, white_in, send_sem, recv_sem, loc_sem) = scratch[chunks:]

    i = lax.axis_index("rows")
    x = lax.axis_index("cols")
    s = lax.axis_index("sub")
    other = 1 - s
    mine = pl.ds(pl.multiple_of(s * half, half), half)
    low = i < n_rows // 2
    mid = jnp.where(low, n_rows // 2 - 1, n_rows // 2)
    end = jnp.where(low, 0, n_rows - 1)
    far_mid, far_end = n_rows - 1 - mid, n_rows - 1 - end
    is_mid = i == mid
    is_end = i == end
    always = i >= 0
    edge = 2
    rest = tile_rows - edge
    in_edge = jnp.where(low, tile_rows - edge, 0)
    in_rest = jnp.where(low, 0, edge)
    out_edge = jnp.where(low, 0, tile_rows - edge)
    below, above = 0, tile_rows + edge
    served_at = jnp.where(low, 0, served)
    theirs_at = served - served_at
    served_cols, theirs_cols = pl.ds(served_at, served), pl.ds(theirs_at, served)
    inner = pl.ds(edge, tile_cols)
    count = {"remote": 0, "local": 0}

    class Remote:
        def __init__(self, sends, receives, src, dst, landed, to):
            self.at, self.sends, self.receives = count["remote"], sends, receives
            self.src, self.dst, self.landed, self.to = src, dst, landed, to
            count["remote"] += 1

        def copy(self, src, dst):
            return pltpu.make_async_remote_copy(
                src_ref=src, dst_ref=dst, send_sem=send_sem.at[self.at], recv_sem=recv_sem.at[self.at],
                device_id=self.to, device_id_type=MESH)

        def start(self):
            @pl.when(self.sends)
            def _():
                self.copy(self.src, self.dst).start()

        def wait_recv(self):
            @pl.when(self.receives)
            def _():
                self.copy(self.landed, self.landed).wait_recv()

        def wait_send(self):
            @pl.when(self.sends)
            def _():
                self.copy(self.src, self.dst).wait_send()

    class Local:
        def __init__(self, here, src, dst):
            self.here = here
            self.copy = pltpu.make_async_copy(src, dst, loc_sem.at[count["local"]])
            count["local"] += 1

        def start(self):
            @pl.when(self.here)
            def _():
                self.copy.start()

        def wait(self):
            @pl.when(self.here)
            def _():
                self.copy.wait()

    def rows_of(tile, first, size):
        return pl.ds(tile * tile_rows + first, size)

    def both_cols(k):
        return pl.ds(starts[k], sizes[k])

    to_partner, to_mid, to_end = {"sub": other}, {"rows": mid}, {"rows": end}
    to_far_mid, to_far_end = {"rows": far_mid}, {"rows": far_end}

    own = [
        Local(always, conv.at[:, :, mine, :], near.at[pl.ds(edge, tile_rows), inner]),
        Local(always, near_factor, near_w.at[s]),
        Local(is_mid, far_factor, far_w.at[s]),
        Local(always, near_codes, near_codes_s.at[s]),
        Local(always, levels, levels_s),
        Local(is_mid, far_codes, far_codes_s.at[i, s]),
        Local(is_mid, conv.at[:, served_cols, mine, :], far_served.at[rows_of(i, 0, tile_rows)]),
    ] + [
        Local(is_mid, conv.at[:, both_cols(k), mine, :], far_both[k].at[rows_of(i, 0, tile_rows)])
        for k in range(chunks)
    ]
    for copy in own:
        copy.start()

    def clear(where, rows, cols):
        @pl.when(where)
        def _():
            near[rows, cols] = jnp.zeros((rows.stop - rows.start, cols.stop - cols.start) + near.shape[2:], near.dtype)

    clear(i == 0, slice(0, edge), slice(0, tile_cols + 2 * edge))
    clear(i == n_rows - 1, slice(above, above + edge), slice(0, tile_cols + 2 * edge))
    clear(x == 0, slice(0, tile_rows + 2 * edge), slice(0, edge))
    clear(x == n_cols - 1, slice(0, tile_rows + 2 * edge), slice(tile_cols + edge, tile_cols + 2 * edge))

    def present(di, dx):
        ok = always
        if di == -1:
            ok = ok & (i > 0)
        if di == 1:
            ok = ok & (i < n_rows - 1)
        if dx == -1:
            ok = ok & (x > 0)
        if dx == 1:
            ok = ok & (x < n_cols - 1)
        return ok

    barrier = pltpu.get_barrier_semaphore()
    for di, dx in ((-1, 0), (1, 0), (0, -1), (0, 1)):
        @pl.when(present(di, dx))
        def _():
            pl.semaphore_signal(barrier, inc=1, device_id={"rows": i + di, "cols": x + dx}, device_id_type=MESH)
    pl.semaphore_signal(barrier, inc=1, device_id=to_partner, device_id_type=MESH)
    count_z = (i > 0).astype(jnp.int32) + (i < n_rows - 1).astype(jnp.int32)
    count_x = (x > 0).astype(jnp.int32) + (x < n_cols - 1).astype(jnp.int32)
    pl.semaphore_wait(barrier, count_z + count_x + 1)

    def exchange(src, dst, landed):
        return Remote(always, always, src, dst, landed, to_partner)

    def inward(src, dst, landed):
        return Remote(is_end, is_mid, src, dst, landed, to_mid)

    def outward(src, dst, landed):
        return Remote(is_mid, is_end, src, dst, landed, to_end)

    def across(src, dst, landed):
        return Remote(is_mid, is_mid, src, dst, landed, to_far_mid)

    def between(src, dst, landed):
        return Remote(is_mid, is_mid, src, dst, landed, to_partner)

    from_inside = pl.ds(jnp.where(low, above, below), edge)
    from_outside = pl.ds(jnp.where(low, below, above), edge)
    edge_rows = conv.at[pl.ds(in_edge, edge), :, mine, :]

    code_near = exchange(near_codes, near_codes_v.at[s], near_codes_v.at[other])
    code_own = between(far_codes, far_codes_v.at[i, s], far_codes_v.at[i, other])
    code_end = inward(far_codes, far_codes_v.at[end, s], far_codes_v.at[end, s])
    code_mid = across(far_codes, far_codes_v.at[mid, s], far_codes_v.at[far_mid, s])
    code_relay = across(far_codes_v.at[end, s], far_codes_v.at[end, s], far_codes_v.at[far_end, s])
    code_share = [
        between(far_codes_v.at[tile, s], far_codes_v.at[tile, s], far_codes_v.at[tile, other])
        for tile in (end, far_mid, far_end)
    ]

    mid_edge = across(edge_rows, near.at[from_outside, inner], near.at[from_inside, inner])
    end_edge = inward(edge_rows, near.at[from_outside, inner], near.at[from_outside, inner])
    back_edge = outward(
        conv.at[pl.ds(out_edge, edge), :, mine, :], near.at[from_inside, inner], near.at[from_inside, inner])

    their_rest = pl.ds(jnp.where(low, edge, 0), rest)

    def rest_of(cols):
        return conv.at[pl.ds(in_rest, rest), cols, mine, :]

    def far_mid_rest(ref):
        return ref.at[pl.ds(far_mid * tile_rows + jnp.where(low, edge, 0), rest)]

    mid_rest = across(
        rest_of(theirs_cols), far_served.at[rows_of(mid, in_rest, rest)], far_mid_rest(far_served))
    mid_rest_both = [
        across(rest_of(both_cols(k)), far_both[k].at[rows_of(mid, in_rest, rest)], far_mid_rest(far_both[k]))
        for k in range(chunks)
    ]

    def end_rest_to(cols, ref):
        return inward(rest_of(cols), ref, ref)

    end_rest_theirs = end_rest_to(theirs_cols, stage.at[pl.ds(in_rest, rest)])
    end_rest_both = [
        end_rest_to(both_cols(k), far_both[k].at[rows_of(end, in_rest, rest)]) for k in range(chunks)
    ]
    end_rest_served = end_rest_to(served_cols, far_served.at[rows_of(end, in_rest, rest)])

    relay_theirs = across(
        stage, far_served.at[rows_of(end, 0, tile_rows)], far_served.at[rows_of(far_end, 0, tile_rows)])
    relay_both = [
        across(
            far_both[k].at[rows_of(end, 0, tile_rows)], far_both[k].at[rows_of(end, 0, tile_rows)],
            far_both[k].at[rows_of(far_end, 0, tile_rows)])
        for k in range(chunks)
    ]

    white_far_end = Remote(
        is_mid, is_end, white_served.at[2], white_in.at[:, served_cols], white_in.at[:, theirs_cols], to_far_end)
    white_far_mid = across(white_served.at[1], white_in.at[:, served_cols], white_in.at[:, theirs_cols])
    white_end = outward(white_served.at[0], white_in.at[:, served_cols], white_in.at[:, served_cols])
    white_end_both = [
        outward(
            white_both.at[:, pl.ds(starts[k] - starts[0], sizes[k])], white_in.at[:, both_cols(k)],
            white_in.at[:, both_cols(k)])
        for k in range(chunks)
    ]

    def side_copy(dx):
        src, dst = (0, tile_cols + edge) if dx == -1 else (tile_cols - edge, 0)
        at = near.at[pl.ds(edge, tile_rows), pl.ds(dst, edge)]
        return Remote(
            present(0, dx), present(0, -dx), conv.at[:, pl.ds(src, edge), mine, :], at, at, {"cols": x + dx})

    sides = [side_copy(dx) for dx in (-1, 1)]

    def corner_copy(di, dx):
        rows = pl.ds(below if di == -1 else above, edge)
        src, dst = (edge, tile_cols + edge) if dx == -1 else (tile_cols, 0)
        at = near.at[rows, pl.ds(dst, edge)]
        return Remote(
            present(di, 0) & present(0, dx), present(di, 0) & present(0, -dx), near.at[rows, pl.ds(src, edge)], at, at,
            {"cols": x + dx})

    corners = [corner_copy(di, dx) for di in (-1, 1) for dx in (-1, 1)]
    factor_near = exchange(near_factor, near_w.at[s], near_w.at[other])
    factor_far = between(far_factor, far_w.at[s], far_w.at[other])

    end_to_far = [
        Local(is_mid, near.at[from_outside, pl.ds(edge + theirs_at, served)], stage.at[pl.ds(in_edge, edge)]),
        Local(is_mid, near.at[from_outside, pl.ds(edge + served_at, served)], far_served.at[rows_of(end, in_edge, edge)]),
    ] + [
        Local(
            is_mid, near.at[from_outside, pl.ds(edge + starts[k], sizes[k])],
            far_both[k].at[rows_of(end, in_edge, edge)])
        for k in range(chunks)
    ]
    their_edge = jnp.where(low, 0, tile_rows - edge)
    mid_to_far = [
        Local(
            is_mid, near.at[from_inside, pl.ds(edge + served_at, served)],
            far_served.at[pl.ds(far_mid * tile_rows + their_edge, edge)]),
    ] + [
        Local(
            is_mid, near.at[from_inside, pl.ds(edge + starts[k], sizes[k])],
            far_both[k].at[pl.ds(far_mid * tile_rows + their_edge, edge)])
        for k in range(chunks)
    ]
    near_codes_in = Local(always, near_codes_v.at[other], near_codes_s.at[other])
    far_codes_in = [Local(is_mid, far_codes_v.at[i, other], far_codes_s.at[i, other])] + [
        Local(is_mid, far_codes_v.at[tile], far_codes_s.at[tile]) for tile in (end, far_mid, far_end)
    ]

    first = [code_end, code_mid, code_near, code_own, mid_edge, end_edge, back_edge] + sides + [factor_near, factor_far]
    for flow in first:
        flow.start()
    end_rest_theirs.start()
    for k in range(chunks):
        end_rest_both[k].start()
    end_rest_served.start()
    code_end.wait_recv()
    code_relay.start()
    mid_rest.start()
    for k in range(chunks):
        mid_rest_both[k].start()
    code_share[0].start()
    code_mid.wait_recv()
    code_share[1].start()
    code_near.wait_recv()
    near_codes_in.start()
    code_own.wait_recv()
    far_codes_in[0].start()

    end_edge.wait_recv()
    for copy in end_to_far:
        copy.start()
    mid_edge.wait_recv()
    back_edge.wait_recv()
    own[0].wait()
    for corner in corners:
        corner.start()
    for copy in mid_to_far:
        copy.start()
    for copy in own[1:]:
        copy.wait()
    for copy in end_to_far:
        copy.wait()
    end_rest_theirs.wait_recv()
    relay_theirs.start()
    near_codes_in.wait()
    for side in sides:
        side.wait_recv()
    factor_near.wait_recv()
    for corner in corners:
        corner.wait_recv()

    contract = (((1,), (1,)), ((), ()))
    part_slots = 2 * near_slots // PARTS

    def block_rows(block):
        return pl.ds(pl.multiple_of(block * half, half), half)

    def pair_rows(block):
        return pl.ds(pl.multiple_of(block * half, 2 * half), 2 * half)

    def joined(first, second):
        both = jnp.concatenate([first.astype(jnp.float32), second.astype(jnp.float32)], axis=0)
        return both.astype(jnp.bfloat16)

    def near_part(part):
        sub, base = part * part_slots // near_slots, part * part_slots % near_slots

        def near_block(r, c, slot):
            code = near_codes_s[sub, r, base + slot, c]
            down = lax.shift_right_logical(code * 205, 10)
            return near[r + down, c + code - 5 * down]

        def gather(c, carry):
            for r in range(0, tile_rows, 2):
                for slot in range(part_slots):
                    near_g[pair_rows(c * tile_rows + r), slot * pixels:(slot + 1) * pixels] = joined(
                        near_block(r, c, slot), near_block(r + 1, c, slot))
            return carry

        lax.fori_loop(0, tile_cols, gather, 0)
        product = lax.dot_general(
            near_g[...], near_w[sub, :, base * pixels:(base + part_slots) * pixels], contract,
            preferred_element_type=jnp.float32)
        if part == 0:
            near_acc[...] = product
        else:
            near_acc[...] += product

    def far_group(blocks, col0, size, targets):
        rows = size * tile_rows * half
        depth = far_slots * pixels

        def body(c, carry):
            for who, (tile, _) in enumerate(targets):
                def far_block(r, sub, slot):
                    return blocks[far_codes_s[tile, sub, r, slot, col0 + c], c]

                for r in range(0, tile_rows, 2):
                    for sub in range(2):
                        for slot in range(far_slots):
                            at = sub * far_slots + slot
                            far_g[pair_rows((who * size + c) * tile_rows + r), at * pixels:(at + 1) * pixels] = joined(
                                far_block(r, sub, slot), far_block(r + 1, sub, slot))
            return carry

        lax.fori_loop(0, size, body, 0)
        total = len(targets) * rows
        product = lax.dot_general(
            far_g[:total, :depth], far_w[0], contract, preferred_element_type=jnp.float32)
        product += lax.dot_general(
            far_g[:total, depth:], far_w[1], contract, preferred_element_type=jnp.float32)
        far_acc[:total, :] = product

        def subtract(c, carry):
            for who, (tile, put) in enumerate(targets):
                for r in range(tile_rows):
                    value = blocks[tile * tile_rows + r, c].astype(jnp.float32)
                    put(r, c, value - far_acc[block_rows((who * size + c) * tile_rows + r), :])
            return carry

        lax.fori_loop(0, size, subtract, 0)

    def fine(r, c):
        return near[edge + r, edge + c].astype(jnp.float32) - near_acc[block_rows(c * tile_rows + r), :]

    def put_own(col0):
        def put(r, c, white):
            out[r, col0 + c] = jnp.where(levels_s[r, col0 + c] == 1, fine(r, col0 + c), white).astype(jnp.bfloat16)
        return put

    def put_served(which):
        def put(r, c, white):
            white_served[which, r, c] = white.astype(jnp.bfloat16)
        return put

    def put_both(col0):
        def put(r, c, white):
            white_both[r, col0 - starts[0] + c] = white.astype(jnp.bfloat16)
        return put

    def finish(first, last):
        def body(c, carry):
            for r in range(tile_rows):
                white = white_in[r, c].astype(jnp.float32)
                out[r, c] = jnp.where(levels_s[r, c] == 1, fine(r, c), white).astype(jnp.bfloat16)
            return carry

        lax.fori_loop(first, last, body, 0)

    @pl.when(is_mid)
    def _():
        near_part(0)
        code_relay.wait_recv()
        code_share[2].start()
        near_part(1)
        for copy in mid_to_far:
            copy.wait()
        for k in range(chunks):
            end_rest_both[k].wait_recv()
            relay_both[k].start()
        for k in range(2, PARTS):
            near_part(k)
        for share in code_share:
            share.wait_recv()
        for copy in far_codes_in[1:]:
            copy.start()
        for copy in far_codes_in:
            copy.wait()
        factor_far.wait_recv()
        mid_rest.wait_recv()
        end_rest_served.wait_recv()
        relay_theirs.wait_recv()
        far_group(far_served, served_at, served, [
            (far_end, put_served(2)), (far_mid, put_served(1)), (end, put_served(0)), (i, put_own(served_at))])
        white_far_end.start()
        white_far_mid.start()
        white_end.start()
        for k in range(chunks):
            mid_rest_both[k].wait_recv()
            relay_both[k].wait_recv()
            far_group(far_both[k], starts[k], sizes[k], [(end, put_both(starts[k])), (i, put_own(starts[k]))])
            white_end_both[k].start()
        white_far_mid.wait_recv()
        finish(theirs_at, theirs_at + served)

    @pl.when(is_end)
    def _():
        for part in range(PARTS):
            near_part(part)
        white_end.wait_recv()
        finish(served_at, served_at + served)
        for k in range(chunks - 1):
            white_end_both[k].wait_recv()
            finish(starts[k], starts[k + 1])
        white_far_end.wait_recv()
        finish(theirs_at, theirs_at + served)
        white_end_both[chunks - 1].wait_recv()
        finish(starts[chunks - 1], starts[chunks])

    for flow in first + [end_rest_theirs] + end_rest_both + [end_rest_served, code_relay, mid_rest] + mid_rest_both:
        flow.wait_send()
    for flow in corners + [relay_theirs] + relay_both + code_share:
        flow.wait_send()
    for flow in [white_far_end, white_far_mid, white_end] + white_end_both:
        flow.wait_send()


def put_out(src, dst, sem):
    pieces = sem.shape[0]
    size = src.shape[0] // pieces
    copies = [
        pltpu.make_async_copy(src.at[pl.ds(k * size, size)], dst.at[pl.ds(k * size, size)], sem.at[k])
        for k in range(pieces)
    ]
    for copy in copies:
        copy.start()
    for copy in copies:
        copy.wait()


def pair_on_device(convergence, block_level, near_codes, far_rows, near_factor, far_factor):
    tile_rows, tile_cols, samples, pixels = convergence.shape
    n_rows, n_cols = lax.axis_size("rows"), lax.axis_size("cols")
    near_slots, far_slots = near_codes.shape[2], far_rows.shape[2]
    half = samples // 2
    served = tile_cols // 4
    starts = group_starts(tile_cols, served)
    sizes = [starts[k + 1] - starts[k] for k in range(len(starts) - 1)]
    near_codes = jnp.transpose(near_codes, (0, 2, 1))
    far_codes = jnp.transpose(far_rows, (0, 2, 1))
    dims = (n_rows, n_cols, tile_rows, tile_cols, half, pixels, near_slots, far_slots, served)
    block = (half, pixels)
    bf16, f32, i32 = jnp.bfloat16, jnp.float32, jnp.int32
    all_rows = tile_rows * tile_cols * half
    group_rows = tile_rows * half * max([n_rows * served] + [2 * size for size in sizes])
    dma = pltpu.SemaphoreType.DMA
    scratch = [pltpu.VMEM((n_rows * tile_rows, size) + block, bf16) for size in sizes]
    scratch += [
        pltpu.VMEM((n_rows * tile_rows, served) + block, bf16),
        pltpu.VMEM((tile_rows + 4, tile_cols + 4) + block, bf16),
        pltpu.VMEM((tile_rows, served) + block, bf16),
        pltpu.VMEM((2,) + near_factor.shape, bf16),
        pltpu.VMEM((2,) + far_factor.shape, bf16),
        pltpu.VMEM((2,) + near_codes.shape, i32),
        pltpu.VMEM((n_rows, 2) + far_codes.shape, i32),
        pltpu.SMEM((2,) + near_codes.shape, i32),
        pltpu.SMEM((n_rows, 2) + far_codes.shape, i32),
        pltpu.SMEM(block_level.shape, i32),
        pltpu.VMEM((all_rows, 2 * near_slots // PARTS * pixels), bf16),
        pltpu.VMEM((group_rows, 2 * far_slots * pixels), bf16),
        pltpu.VMEM((all_rows, pixels), f32),
        pltpu.VMEM((group_rows, pixels), f32),
        pltpu.VMEM((3, tile_rows, served) + block, bf16),
        pltpu.VMEM((tile_rows, tile_cols - 2 * served) + block, bf16),
        pltpu.VMEM((tile_rows, tile_cols) + block, bf16),
        dma((26 + 4 * len(sizes),)),
        dma((26 + 4 * len(sizes),)),
        dma((16 + 3 * len(sizes),)),
    ]
    anywhere = pl.BlockSpec(memory_space=pl.ANY)
    vmem = pl.BlockSpec(memory_space=pltpu.VMEM)
    white = pl.pallas_call(
        functools.partial(pair_kernel, dims),
        out_shape=pltpu.VMEM((tile_rows, tile_cols) + block, bf16),
        in_specs=[anywhere] * 6,
        out_specs=vmem,
        scratch_shapes=scratch,
        compiler_params=pltpu.CompilerParams(
            collective_id=0, has_side_effects=True, vmem_limit_bytes=56 * 1024 * 1024),
    )(convergence, near_codes, far_codes, block_level, near_factor, far_factor)
    return pl.pallas_call(
        put_out,
        out_shape=jax.ShapeDtypeStruct(white.shape, bf16),
        in_specs=[vmem],
        out_specs=anywhere,
        scratch_shapes=[dma((tile_rows,))],
    )(pltpu.with_memory_space_constraint(white, pltpu.VMEM))


def solution(mesh):
    placed = (
        P(("fields", "rows"), "cols", None, None),
        P(("fields", "rows"), "cols"),
        P(("fields", "rows"), "cols", "sub"),
        P(("fields", "rows"), "cols", "sub"),
        P(None, "sub"),
        P(None, "sub"),
    )
    two_middle_tiles = mesh.shape["rows"] - 2 == 2
    return jax.shard_map(
        pair_on_device if two_middle_tiles else on_device,
        mesh=mesh,
        in_specs=placed,
        out_specs=P(("fields", "rows"), "cols", "sub", None),
        check_vma=False,
    )
```

```python
import functools

import jax
import jax.numpy as jnp
from jax import lax
from jax.experimental import pallas as pl
from jax.experimental.pallas import tpu as pltpu
from jax.sharding import PartitionSpec as P

MESH = pl.DeviceIdType.MESH
PARTS = 4


def chunk_starts(cols):
    return [0, cols * 5 // 16, cols * 10 // 16, cols * 14 // 16, cols]


def kernel(dims, conv, codes, near_factor, far_factor, out, *scratch):
    n_rows, n_cols, tile_rows, tile_cols, half, pixels, near_slots, far_slots = dims
    starts = chunk_starts(tile_cols)
    chunks = len(starts) - 1
    sizes = [starts[k + 1] - starts[k] for k in range(chunks)]
    far = scratch[:chunks]
    (near, near_w, far_w, codes_v, codes_s, near_g, far_g, near_acc, far_acc, end_acc,
     white_src, white_dst, tile_send, tile_recv, white_send, white_recv,
     side_send, side_recv, corner_send, corner_recv, code_send, code_recv, fac_send, fac_recv, loc_sem, halo_sem) = scratch[chunks:]

    i = lax.axis_index("rows")
    x = lax.axis_index("cols")
    s = lax.axis_index("sub")
    other = 1 - s
    mine = pl.ds(pl.multiple_of(s * half, half), half)
    is_end = (i == 0) | (i == n_rows - 1)
    is_mid = (i > 0) & (i < n_rows - 1)
    low_helper = i == 1
    high_helper = i == n_rows - 2
    is_helper = low_helper | high_helper
    end_tile = jnp.where(low_helper, 0, n_rows - 1)
    to_mid = jnp.where(i == 0, 1, n_rows - 2)

    def cols_of(k):
        return pl.ds(starts[k], sizes[k])

    local = [
        pltpu.make_async_copy(
            conv.at[:, :, mine, :],
            near.at[pl.ds(2, tile_rows), pl.ds(2, tile_cols)],
            loc_sem.at[0],
        ),
        pltpu.make_async_copy(near_factor, near_w.at[s], loc_sem.at[1]),
        pltpu.make_async_copy(far_factor, far_w.at[s], loc_sem.at[2]),
        pltpu.make_async_copy(codes, codes_s.at[0, s], loc_sem.at[3]),
    ]
    for copy in local:
        copy.start()
    own_far = [
        pltpu.make_async_copy(
            conv.at[:, cols_of(k), mine, :],
            far[k].at[pl.ds(i * tile_rows, tile_rows)],
            loc_sem.at[6 + k],
        )
        for k in range(chunks)
    ]

    @pl.when(is_mid)
    def _():
        for copy in own_far:
            copy.start()

    @pl.when(i == 0)
    def _():
        near[0:2] = jnp.zeros((2,) + near.shape[1:], near.dtype)

    @pl.when(i == n_rows - 1)
    def _():
        near[tile_rows + 2:tile_rows + 4] = jnp.zeros((2,) + near.shape[1:], near.dtype)

    @pl.when(x == 0)
    def _():
        near[:, 0:2] = jnp.zeros((near.shape[0], 2) + near.shape[2:], near.dtype)

    @pl.when(x == n_cols - 1)
    def _():
        near[:, tile_cols + 2:tile_cols + 4] = jnp.zeros((near.shape[0], 2) + near.shape[2:], near.dtype)

    barrier = pltpu.get_barrier_semaphore()
    offsets = [(-1, 0), (1, 0), (0, -1), (0, 1)]

    def present(di, dx):
        ok = jnp.bool_(True)
        if di == -1:
            ok = ok & (i > 0)
        if di == 1:
            ok = ok & (i < n_rows - 1)
        if dx == -1:
            ok = ok & (x > 0)
        if dx == 1:
            ok = ok & (x < n_cols - 1)
        return ok

    for di, dx in offsets:
        @pl.when(present(di, dx))
        def _():
            pl.semaphore_signal(barrier, inc=1, device_id={"rows": i + di, "cols": x + dx}, device_id_type=MESH)
    pl.semaphore_signal(barrier, inc=1, device_id={"sub": other}, device_id_type=MESH)
    count_z = (i > 0).astype(jnp.int32) + (i < n_rows - 1).astype(jnp.int32)
    count_x = (x > 0).astype(jnp.int32) + (x < n_cols - 1).astype(jnp.int32)
    pl.semaphore_wait(barrier, count_z + count_x + 1)

    def code_copy(which, slot, target):
        return pltpu.make_async_remote_copy(
            src_ref=codes if which < 2 else codes_v.at[slot, s], dst_ref=codes_v.at[slot, s],
            send_sem=code_send.at[which], recv_sem=code_recv.at[which], device_id=target, device_id_type=MESH)

    code_partner = code_copy(0, 0, {"sub": other})
    code_straight = code_copy(1, 1, {"rows": to_mid})
    code_relay = code_copy(2, 1, {"sub": other})
    code_partner.start()

    @pl.when(is_end)
    def _():
        code_straight.start()

    def side_copy(di, dx):
        if di == 0:
            rows_src, rows_dst = pl.ds(0, tile_rows), pl.ds(2, tile_rows)
        elif di == -1:
            rows_src, rows_dst = pl.ds(0, 2), pl.ds(tile_rows + 2, 2)
        else:
            rows_src, rows_dst = pl.ds(tile_rows - 2, 2), pl.ds(0, 2)
        if dx == 0:
            cols_src, cols_dst = pl.ds(0, tile_cols), pl.ds(2, tile_cols)
        elif dx == -1:
            cols_src, cols_dst = pl.ds(0, 2), pl.ds(tile_cols + 2, 2)
        else:
            cols_src, cols_dst = pl.ds(tile_cols - 2, 2), pl.ds(0, 2)
        which = offsets.index((di, dx))
        return pltpu.make_async_remote_copy(
            src_ref=conv.at[rows_src, cols_src, mine, :],
            dst_ref=near.at[rows_dst, cols_dst],
            send_sem=side_send.at[which], recv_sem=side_recv.at[which],
            device_id={"rows": i + di, "cols": x + dx}, device_id_type=MESH)

    def side_sends(di, dx):
        if dx == 0:
            return low_helper if di == -1 else high_helper
        return present(di, dx)

    def side_receives(di, dx):
        if dx == 0:
            return (i == 0) if di == -1 else (i == n_rows - 1)
        return present(-di, -dx)

    def tile_copy(way, d, k, tile):
        src = conv.at[:, cols_of(k), mine, :] if d == 0 else far[k].at[pl.ds(tile * tile_rows, tile_rows)]
        return pltpu.make_async_remote_copy(
            src_ref=src, dst_ref=far[k].at[pl.ds(tile * tile_rows, tile_rows)],
            send_sem=tile_send.at[way, d, k], recv_sem=tile_recv.at[way, d, k],
            device_id={"rows": i - 1 if way == 0 else i + 1}, device_id_type=MESH)

    def sent(way, d, k):
        return tile_copy(way, d, k, i + d if way == 0 else i - d)

    def received(way, d, k):
        return tile_copy(way, d, k, i + 1 + d if way == 0 else i - 1 - d)

    def tile_sends(way, d):
        if way == 0:
            return (i >= 2) & (i + d <= n_rows - 1)
        return (i <= n_rows - 3) & (i - d >= 0)

    def tile_receives(way, d):
        if way == 0:
            return is_mid & (i + 1 + d <= n_rows - 1)
        return is_mid & (i - 1 - d >= 0)

    for k in range(chunks):
        for way in (0, 1):
            @pl.when(tile_sends(way, 0))
            def _():
                sent(way, 0, k).start()
        if k == 0:
            for di, dx in offsets:
                @pl.when(side_sends(di, dx))
                def _():
                    side_copy(di, dx).start()

    def factor_copy(which):
        src, dst = ((near_factor, near_w), (far_factor, far_w))[which]
        return pltpu.make_async_remote_copy(
            src_ref=src, dst_ref=dst.at[s], send_sem=fac_send.at[which],
            recv_sem=fac_recv.at[which], device_id={"sub": other}, device_id_type=MESH)

    for which in (0, 1):
        factor_copy(which).start()

    def halo_copy(way, k):
        if way == 0:
            src_rows, dst_rows = pl.ds((i + 1) * tile_rows, 2), pl.ds(tile_rows + 2, 2)
        else:
            src_rows, dst_rows = pl.ds(i * tile_rows - 2, 2), pl.ds(0, 2)
        return pltpu.make_async_copy(
            far[k].at[src_rows], near.at[dst_rows, pl.ds(2 + starts[k], sizes[k])], halo_sem.at[way, k])

    for d in range(n_rows - 3):
        for k in range(chunks):
            for way in (0, 1):
                @pl.when(tile_receives(way, d))
                def _():
                    received(way, d, k).wait_recv()
                    if d == 0:
                        halo_copy(way, k).start()

                @pl.when(tile_sends(way, d + 1))
                def _():
                    sent(way, d + 1, k).start()

    code_copy(0, 0, {"sub": other}).wait_recv()
    code_in = pltpu.make_async_copy(codes_v.at[0, other], codes_s.at[0, other], loc_sem.at[4])
    code_in.start()
    end_codes = pltpu.make_async_copy(codes_v.at[1], codes_s.at[1], loc_sem.at[5])

    @pl.when(is_helper)
    def _():
        code_straight.wait_recv()
        code_relay.start()

    for copy in local:
        copy.wait()

    @pl.when(is_mid)
    def _():
        for k in range(chunks):
            halo_copy(0, k).wait()
            halo_copy(1, k).wait()
            own_far[k].wait()

    for di, dx in offsets:
        @pl.when(side_receives(di, dx))
        def _():
            side_copy(di, dx).wait_recv()

    def corner_copy(di, dx):
        rows = pl.ds(0, 2) if di == -1 else pl.ds(tile_rows + 2, 2)
        src, dst = (2, tile_cols + 2) if dx == -1 else (tile_cols, 0)
        which = (di + 1) + (dx + 1) // 2
        return pltpu.make_async_remote_copy(
            src_ref=near.at[rows, pl.ds(src, 2)], dst_ref=near.at[rows, pl.ds(dst, 2)],
            send_sem=corner_send.at[which], recv_sem=corner_recv.at[which],
            device_id={"cols": x + dx}, device_id_type=MESH)

    corners = [(di, dx) for di in (-1, 1) for dx in (-1, 1)]
    for di, dx in corners:
        @pl.when(present(di, 0) & present(0, dx))
        def _():
            corner_copy(di, dx).start()

    @pl.when(is_helper)
    def _():
        code_relay.wait_recv()
        end_codes.start()
        end_codes.wait()

    code_in.wait()
    for which in (0, 1):
        factor_copy(which).wait_recv()
    for di, dx in corners:
        @pl.when(present(di, 0) & present(0, -dx))
        def _():
            corner_copy(di, dx).wait_recv()

    contract = (((1,), (1,)), ((), ()))
    part_slots = 2 * near_slots // PARTS

    def block_rows(block):
        return pl.ds(pl.multiple_of(block * half, half), half)

    def pair_rows(block):
        return pl.ds(pl.multiple_of(block * half, 2 * half), 2 * half)

    def joined(first, second):
        both = jnp.concatenate([first.astype(jnp.float32), second.astype(jnp.float32)], axis=0)
        return both.astype(jnp.bfloat16)

    def near_part(part):
        sub, base = part * part_slots // near_slots, part * part_slots % near_slots

        def near_block(r, c, slot):
            code = codes_s[0, sub, r, base + slot, c]
            down = lax.shift_right_logical(code * 205, 10)
            return near[r + down, c + code - 5 * down]

        def gather(c, carry):
            for r in range(0, tile_rows, 2):
                for slot in range(part_slots):
                    near_g[pair_rows(c * tile_rows + r), slot * pixels:(slot + 1) * pixels] = joined(
                        near_block(r, c, slot), near_block(r + 1, c, slot))
            return carry

        lax.fori_loop(0, tile_cols, gather, 0)
        product = lax.dot_general(
            near_g[...], near_w[sub, :, base * pixels:(base + part_slots) * pixels], contract,
            preferred_element_type=jnp.float32)
        if part == 0:
            near_acc[...] = product
        else:
            near_acc[...] += product

    level_at = near_slots + far_slots

    def far_chunk(k):
        rows = sizes[k] * tile_rows * half

        def gather_far(who):
            def far_block(r, c, sub, slot):
                row = codes_s[who, sub, r, near_slots + slot, starts[k] + c]
                return far[k][row, c]

            def body(c, carry):
                for r in range(0, tile_rows, 2):
                    for sub in range(2):
                        for slot in range(far_slots):
                            at = sub * far_slots + slot
                            far_g[pair_rows((who * sizes[k] + c) * tile_rows + r), at * pixels:(at + 1) * pixels] = joined(
                                far_block(r, c, sub, slot), far_block(r + 1, c, sub, slot))
                return carry

            lax.fori_loop(0, sizes[k], body, 0)

        gather_far(0)

        @pl.when(is_helper)
        def _():
            gather_far(1)

        depth = far_slots * pixels
        product = lax.dot_general(
            far_g[:2 * rows, :depth], far_w[0], contract, preferred_element_type=jnp.float32)
        product += lax.dot_general(
            far_g[:2 * rows, depth:], far_w[1], contract, preferred_element_type=jnp.float32)
        far_acc[pl.ds(starts[k] * tile_rows * half, rows), :] = product[:rows]
        end_acc[pl.ds(0, rows), :] = product[rows:]

        @pl.when(is_helper)
        def _():
            def body(c, carry):
                for r in range(tile_rows):
                    value = far[k][end_tile * tile_rows + r, c].astype(jnp.float32)
                    white_src[r, starts[k] + c] = (value - end_acc[block_rows(c * tile_rows + r), :]).astype(jnp.bfloat16)
                return carry

            lax.fori_loop(0, sizes[k], body, 0)
            white_copy(k).start()

    def white_copy(k):
        return pltpu.make_async_remote_copy(
            src_ref=white_src.at[:, cols_of(k)], dst_ref=white_dst.at[:, cols_of(k)],
            send_sem=white_send.at[k], recv_sem=white_recv.at[k],
            device_id={"rows": end_tile}, device_id_type=MESH)

    @pl.when(is_mid)
    def _():
        near_part(0)
        for k in range(chunks):
            d = n_rows - 3
            for way in (0, 1):
                @pl.when(tile_receives(way, d))
                def _():
                    received(way, d, k).wait_recv()
            far_chunk(k)
            if k < PARTS - 2:
                near_part(k + 1)
        near_part(PARTS - 1)

        def body(c, carry):
            for r in range(tile_rows):
                level = codes_s[0, s, r, level_at, c]
                at = block_rows(c * tile_rows + r)
                mean = jnp.where(level == 1, near_acc[at, :], far_acc[at, :])
                out[r, c] = (near[2 + r, 2 + c].astype(jnp.float32) - mean).astype(jnp.bfloat16)
            return carry

        lax.fori_loop(0, tile_cols, body, 0)

    @pl.when(is_end)
    def _():
        for part in range(PARTS):
            near_part(part)
        for k in range(chunks):
            white_copy(k).wait_recv()

            def body(c, carry):
                for r in range(tile_rows):
                    level = codes_s[0, s, r, level_at, c]
                    mean = near_acc[block_rows(c * tile_rows + r), :]
                    fine = near[2 + r, 2 + c].astype(jnp.float32) - mean
                    coarse = white_dst[r, c].astype(jnp.float32)
                    out[r, c] = jnp.where(level == 1, fine, coarse).astype(jnp.bfloat16)
                return carry

            lax.fori_loop(starts[k], starts[k + 1], body, 0)

    code_partner.wait_send()

    @pl.when(is_end)
    def _():
        code_straight.wait_send()

    for di, dx in corners:
        @pl.when(present(di, 0) & present(0, dx))
        def _():
            corner_copy(di, dx).wait_send()

    for di, dx in offsets:
        @pl.when(side_sends(di, dx))
        def _():
            side_copy(di, dx).wait_send()
    for which in (0, 1):
        factor_copy(which).wait_send()
    for d in range(n_rows - 2):
        for way in (0, 1):
            @pl.when(tile_sends(way, d))
            def _():
                for k in range(chunks):
                    sent(way, d, k).wait_send()

    @pl.when(is_helper)
    def _():
        code_relay.wait_send()
        for k in range(chunks):
            white_copy(k).wait_send()


def on_device(convergence, block_level, near_codes, far_rows, near_factor, far_factor):
    tile_rows, tile_cols, samples, pixels = convergence.shape
    n_rows, n_cols = lax.axis_size("rows"), lax.axis_size("cols")
    near_slots, far_slots = near_codes.shape[2], far_rows.shape[2]
    half = samples // 2
    starts = chunk_starts(tile_cols)
    chunks = len(starts) - 1
    codes = jnp.concatenate(
        [jnp.transpose(near_codes, (0, 2, 1)), jnp.transpose(far_rows, (0, 2, 1)), block_level[:, None, :]], axis=1)
    dims = (n_rows, n_cols, tile_rows, tile_cols, half, pixels, near_slots, far_slots)
    block = (half, pixels)
    bf16, f32 = jnp.bfloat16, jnp.float32
    all_rows = tile_rows * tile_cols * half
    chunk_rows = tile_rows * half * max(starts[k + 1] - starts[k] for k in range(chunks))
    dma = pltpu.SemaphoreType.DMA
    scratch = [pltpu.VMEM((n_rows * tile_rows, starts[k + 1] - starts[k]) + block, bf16) for k in range(chunks)]
    scratch += [
        pltpu.VMEM((tile_rows + 4, tile_cols + 4) + block, bf16),
        pltpu.VMEM((2,) + near_factor.shape, bf16),
        pltpu.VMEM((2,) + far_factor.shape, bf16),
        pltpu.VMEM((2, 2) + codes.shape, jnp.int32),
        pltpu.SMEM((2, 2) + codes.shape, jnp.int32),
        pltpu.VMEM((all_rows, 2 * near_slots // PARTS * pixels), bf16),
        pltpu.VMEM((2 * chunk_rows, 2 * far_slots * pixels), bf16),
        pltpu.VMEM((all_rows, pixels), f32),
        pltpu.VMEM((all_rows, pixels), f32),
        pltpu.VMEM((chunk_rows, pixels), f32),
        pltpu.VMEM((tile_rows, tile_cols) + block, bf16),
        pltpu.VMEM((tile_rows, tile_cols) + block, bf16),
        dma((2, n_rows - 2, chunks)),
        dma((2, n_rows - 2, chunks)),
        dma((chunks,)),
        dma((chunks,)),
        dma((4,)),
        dma((4,)),
        dma((4,)),
        dma((4,)),
        dma((3,)),
        dma((3,)),
        dma((2,)),
        dma((2,)),
        dma((6 + chunks,)),
        dma((2, chunks)),
    ]
    anywhere = pl.BlockSpec(memory_space=pl.ANY)
    vmem = pl.BlockSpec(memory_space=pltpu.VMEM)
    return pl.pallas_call(
        functools.partial(kernel, dims),
        out_shape=jax.ShapeDtypeStruct((tile_rows, tile_cols) + block, bf16),
        in_specs=[anywhere, vmem, anywhere, anywhere],
        out_specs=vmem,
        scratch_shapes=scratch,
        compiler_params=pltpu.CompilerParams(
            collective_id=0, has_side_effects=True, vmem_limit_bytes=56 * 1024 * 1024),
    )(convergence, codes, near_factor, far_factor)


def group_starts(cols, served):
    left = cols - 2 * served
    return [2 * served, 2 * served + left // 2, 2 * served + left * 3 // 4, cols]


def pair_kernel(dims, conv, near_codes, far_codes, levels, near_factor, far_factor, out, *scratch):
    n_rows, n_cols, tile_rows, tile_cols, half, pixels, near_slots, far_slots, served = dims
    starts = group_starts(tile_cols, served)
    chunks = len(starts) - 1
    sizes = [starts[k + 1] - starts[k] for k in range(chunks)]
    far_both = scratch[:chunks]
    (far_served, near, stage, bits, near_w, far_w, near_codes_v, far_codes_v, near_codes_s, far_codes_s, levels_s,
     near_g, far_g, near_acc, far_acc, white_served, white_both, white_own, white_in, send_sem, recv_sem, loc_sem) = scratch[chunks:]

    i = lax.axis_index("rows")
    x = lax.axis_index("cols")
    s = lax.axis_index("sub")
    other = 1 - s
    mine = pl.ds(pl.multiple_of(s * half, half), half)
    low = i < n_rows // 2
    mid = jnp.where(low, n_rows // 2 - 1, n_rows // 2)
    end = jnp.where(low, 0, n_rows - 1)
    far_mid, far_end = n_rows - 1 - mid, n_rows - 1 - end
    is_mid = i == mid
    is_end = i == end
    always = i >= 0
    edge = 2
    rest = tile_rows - edge
    in_edge = jnp.where(low, tile_rows - edge, 0)
    in_rest = jnp.where(low, 0, edge)
    out_edge = jnp.where(low, 0, tile_rows - edge)
    below, above = 0, tile_rows + edge
    served_at = jnp.where(low, 0, served)
    theirs_at = served - served_at
    served_cols, theirs_cols = pl.ds(served_at, served), pl.ds(theirs_at, served)
    inner = pl.ds(edge, tile_cols)
    count = {"remote": 0, "local": 0}

    class Remote:
        def __init__(self, sends, receives, src, dst, landed, to):
            self.at, self.sends, self.receives = count["remote"], sends, receives
            self.src, self.dst, self.landed, self.to = src, dst, landed, to
            count["remote"] += 1

        def copy(self, src, dst):
            return pltpu.make_async_remote_copy(
                src_ref=src, dst_ref=dst, send_sem=send_sem.at[self.at], recv_sem=recv_sem.at[self.at],
                device_id=self.to, device_id_type=MESH)

        def start(self):
            @pl.when(self.sends)
            def _():
                self.copy(self.src, self.dst).start()

        def wait_recv(self):
            @pl.when(self.receives)
            def _():
                self.copy(self.landed, self.landed).wait_recv()

        def wait_send(self):
            @pl.when(self.sends)
            def _():
                self.copy(self.src, self.dst).wait_send()

    class Local:
        def __init__(self, here, src, dst):
            self.here = here
            self.copy = pltpu.make_async_copy(src, dst, loc_sem.at[count["local"]])
            count["local"] += 1

        def start(self):
            @pl.when(self.here)
            def _():
                self.copy.start()

        def wait(self):
            @pl.when(self.here)
            def _():
                self.copy.wait()

    def rows_of(tile, first, size):
        return pl.ds(tile * tile_rows + first, size)

    def both_cols(k):
        return pl.ds(starts[k], sizes[k])

    to_partner, to_mid, to_end = {"sub": other}, {"rows": mid}, {"rows": end}
    to_far_mid, to_far_end = {"rows": far_mid}, {"rows": far_end}

    own = [
        Local(always, conv.at[:, :, mine, :], near.at[pl.ds(edge, tile_rows), inner]),
        Local(always, near_factor, near_w.at[s]),
        Local(is_mid, far_factor, far_w.at[s]),
        Local(always, near_codes, near_codes_s.at[s]),
        Local(always, levels, levels_s),
        Local(is_mid, far_codes, far_codes_s.at[i, s]),
        Local(is_mid, conv.at[:, served_cols, mine, :], far_served.at[rows_of(i, 0, tile_rows)]),
    ] + [
        Local(is_mid, conv.at[:, both_cols(k), mine, :], far_both[k].at[rows_of(i, 0, tile_rows)])
        for k in range(chunks)
    ]
    for copy in own:
        copy.start()

    def clear(where, rows, cols):
        @pl.when(where)
        def _():
            near[rows, cols] = jnp.zeros((rows.stop - rows.start, cols.stop - cols.start) + near.shape[2:], near.dtype)

    clear(i == 0, slice(0, edge), slice(0, tile_cols + 2 * edge))
    clear(i == n_rows - 1, slice(above, above + edge), slice(0, tile_cols + 2 * edge))
    clear(x == 0, slice(0, tile_rows + 2 * edge), slice(0, edge))
    clear(x == n_cols - 1, slice(0, tile_rows + 2 * edge), slice(tile_cols + edge, tile_cols + 2 * edge))

    def present(di, dx):
        ok = always
        if di == -1:
            ok = ok & (i > 0)
        if di == 1:
            ok = ok & (i < n_rows - 1)
        if dx == -1:
            ok = ok & (x > 0)
        if dx == 1:
            ok = ok & (x < n_cols - 1)
        return ok

    barrier = pltpu.get_barrier_semaphore()
    for di, dx in ((-1, 0), (1, 0), (0, -1), (0, 1)):
        @pl.when(present(di, dx))
        def _():
            pl.semaphore_signal(barrier, inc=1, device_id={"rows": i + di, "cols": x + dx}, device_id_type=MESH)
    pl.semaphore_signal(barrier, inc=1, device_id=to_partner, device_id_type=MESH)
    count_z = (i > 0).astype(jnp.int32) + (i < n_rows - 1).astype(jnp.int32)
    count_x = (x > 0).astype(jnp.int32) + (x < n_cols - 1).astype(jnp.int32)
    pl.semaphore_wait(barrier, count_z + count_x + 1)

    def exchange(src, dst, landed):
        return Remote(always, always, src, dst, landed, to_partner)

    def inward(src, dst, landed):
        return Remote(is_end, is_mid, src, dst, landed, to_mid)

    def outward(src, dst, landed):
        return Remote(is_mid, is_end, src, dst, landed, to_end)

    def across(src, dst, landed):
        return Remote(is_mid, is_mid, src, dst, landed, to_far_mid)

    def between(src, dst, landed):
        return Remote(is_mid, is_mid, src, dst, landed, to_partner)

    from_inside = pl.ds(jnp.where(low, above, below), edge)
    from_outside = pl.ds(jnp.where(low, below, above), edge)
    late_cols = pl.ds(starts[1], tile_cols - starts[1])

    code_near = exchange(near_codes, near_codes_v.at[s], near_codes_v.at[other])
    code_own = between(far_codes, far_codes_v.at[i, s], far_codes_v.at[i, other])
    code_end = inward(far_codes, far_codes_v.at[end, s], far_codes_v.at[end, s])
    code_mid = across(far_codes, far_codes_v.at[mid, s], far_codes_v.at[far_mid, s])
    code_relay = across(far_codes_v.at[end, s], far_codes_v.at[end, s], far_codes_v.at[far_end, s])
    code_share = [
        between(far_codes_v.at[tile, s], far_codes_v.at[tile, s], far_codes_v.at[tile, other])
        for tile in (end, far_mid, far_end)
    ]

    def halo(rows, first, size):
        return near.at[rows, pl.ds(edge + first, size)]

    def in_edge_of(cols):
        return conv.at[pl.ds(in_edge, edge), cols, mine, :]

    def all_rows_of(cols):
        return conv.at[:, cols, mine, :]

    def tile_of(ref, tile):
        return ref.at[rows_of(tile, 0, tile_rows)]

    back_edge = outward(
        conv.at[pl.ds(out_edge, edge), :, mine, :], near.at[from_inside, inner], near.at[from_inside, inner])
    mid_theirs = across(all_rows_of(theirs_cols), tile_of(far_served, mid), tile_of(far_served, far_mid))
    mid_first = across(all_rows_of(both_cols(0)), tile_of(far_both[0], mid), tile_of(far_both[0], far_mid))
    edge_served = across(
        in_edge_of(served_cols), halo(from_outside, served_at, served), halo(from_inside, theirs_at, served))
    edge_late = across(
        in_edge_of(late_cols), halo(from_outside, late_cols.start, late_cols.size),
        halo(from_inside, late_cols.start, late_cols.size))
    their_rest = jnp.where(low, edge, 0)
    mid_rest = [
        across(
            conv.at[pl.ds(in_rest, rest), both_cols(k), mine, :], far_both[k].at[rows_of(mid, in_rest, rest)],
            far_both[k].at[rows_of(far_mid, their_rest, rest)])
        for k in range(1, chunks)
    ]

    def end_to(cols, ref):
        return inward(all_rows_of(cols), ref, ref)

    end_theirs = end_to(theirs_cols, stage)
    end_served = end_to(served_cols, tile_of(far_served, end))
    end_both = [end_to(both_cols(k), tile_of(far_both[k], end)) for k in range(chunks)]
    relay_theirs = across(stage, tile_of(far_served, end), tile_of(far_served, far_end))
    relay_both = [
        across(tile_of(far_both[k], end), tile_of(far_both[k], end), tile_of(far_both[k], far_end))
        for k in range(chunks)
    ]

    white_far_end = Remote(
        is_mid, is_end, white_served.at[2], white_in.at[:, served_cols], white_in.at[:, theirs_cols], to_far_end)
    white_far_mid = across(white_served.at[1], white_in.at[:, served_cols], white_in.at[:, theirs_cols])
    white_end = outward(white_served.at[0], white_in.at[:, served_cols], white_in.at[:, served_cols])
    white_end_both = [
        outward(
            white_both.at[:, pl.ds(starts[k] - starts[0], sizes[k])], white_in.at[:, both_cols(k)],
            white_in.at[:, both_cols(k)])
        for k in range(chunks)
    ]

    def side_copy(dx):
        src, dst = (0, tile_cols + edge) if dx == -1 else (tile_cols - edge, 0)
        at = near.at[pl.ds(edge, tile_rows), pl.ds(dst, edge)]
        return Remote(
            present(0, dx), present(0, -dx), conv.at[:, pl.ds(src, edge), mine, :], at, at, {"cols": x + dx})

    sides = [side_copy(dx) for dx in (-1, 1)]

    def bit_of(di, dx):
        return bits.at[di + 1 + (dx + 1) // 2]

    def bit_copy(di, dx):
        src = conv.at[
            pl.ds(0 if di == -1 else tile_rows - edge, edge), pl.ds(0 if dx == -1 else tile_cols - edge, edge), mine, :]
        return Remote(
            present(di, 0) & present(0, dx), present(-di, 0) & present(0, dx), src, bit_of(-di, dx), bit_of(-di, dx),
            {"rows": i + di})

    def corner_copy(di, dx):
        at = near.at[pl.ds(below if di == -1 else above, edge), pl.ds(tile_cols + edge if dx == -1 else 0, edge)]
        return Remote(
            present(di, 0) & present(0, dx), present(di, 0) & present(0, -dx), bit_of(di, dx), at, at, {"cols": x + dx})

    diagonals = [(di, dx) for di in (-1, 1) for dx in (-1, 1)]
    bit_flows = {(-di, dx): bit_copy(di, dx) for di, dx in diagonals}
    corners = {(di, dx): corner_copy(di, dx) for di, dx in diagonals}
    factor_near = exchange(near_factor, near_w.at[s], near_w.at[other])
    factor_far = between(far_factor, far_w.at[s], far_w.at[other])

    their_edge = jnp.where(low, 0, tile_rows - edge)
    end_halos = [
        Local(is_mid, stage.at[pl.ds(in_edge, edge)], halo(from_outside, theirs_at, served)),
        Local(is_mid, far_served.at[rows_of(end, in_edge, edge)], halo(from_outside, served_at, served)),
    ] + [
        Local(is_mid, far_both[k].at[rows_of(end, in_edge, edge)], halo(from_outside, starts[k], sizes[k]))
        for k in range(chunks)
    ]
    mid_halos = [
        Local(is_mid, far_served.at[rows_of(far_mid, their_edge, edge)], halo(from_inside, served_at, served)),
        Local(is_mid, far_both[0].at[rows_of(far_mid, their_edge, edge)], halo(from_inside, starts[0], sizes[0])),
    ]
    late_edges = [
        Local(is_mid, halo(from_inside, starts[k], sizes[k]), far_both[k].at[rows_of(far_mid, their_edge, edge)])
        for k in range(1, chunks)
    ]
    near_codes_in = Local(always, near_codes_v.at[other], near_codes_s.at[other])
    far_codes_in = [Local(is_mid, far_codes_v.at[i, other], far_codes_s.at[i, other])] + [
        Local(is_mid, far_codes_v.at[tile], far_codes_s.at[tile]) for tile in (end, far_mid, far_end)
    ]

    small = [code_end, code_mid] + [bit_flows[d] for d in diagonals] + [code_near, code_own]
    large = [mid_theirs, end_theirs, mid_first, end_both[0], back_edge, end_served] + end_both[1:]
    factors = [factor_far, factor_near]
    for flow in small + large + sides + factors:
        flow.start()
    code_end.wait_recv()
    code_relay.start()
    code_share[0].start()
    for d in diagonals:
        bit_flows[d].wait_recv()
        corners[d].start()
    code_mid.wait_recv()
    code_share[1].start()
    code_near.wait_recv()
    near_codes_in.start()
    code_own.wait_recv()
    far_codes_in[0].start()
    for copy in own:
        copy.wait()
    near_codes_in.wait()
    for side in sides:
        side.wait_recv()
    for d in diagonals:
        corners[d].wait_recv()

    end_theirs.wait_recv()
    relay_theirs.start()
    end_halos[0].start()
    end_both[0].wait_recv()
    relay_both[0].start()
    edge_served.start()
    edge_late.start()
    for flow in mid_rest:
        flow.start()
    end_halos[2].start()
    code_relay.wait_recv()
    code_share[2].start()
    for share in code_share:
        share.wait_recv()
    for copy in far_codes_in[1:]:
        copy.start()
    for copy in far_codes_in:
        copy.wait()
    for factor in factors:
        factor.wait_recv()

    contract = (((1,), (1,)), ((), ()))
    part_slots = 2 * near_slots // PARTS

    def block_rows(block):
        return pl.ds(pl.multiple_of(block * half, half), half)

    def pair_rows(block):
        return pl.ds(pl.multiple_of(block * half, 2 * half), 2 * half)

    def joined(first, second):
        both = jnp.concatenate([first.astype(jnp.float32), second.astype(jnp.float32)], axis=0)
        return both.astype(jnp.bfloat16)

    def near_part(part):
        sub, base = part * part_slots // near_slots, part * part_slots % near_slots

        def near_block(r, c, slot):
            code = near_codes_s[sub, r, base + slot, c]
            down = lax.shift_right_logical(code * 205, 10)
            return near[r + down, c + code - 5 * down]

        def gather(c, carry):
            for r in range(0, tile_rows, 2):
                for slot in range(part_slots):
                    near_g[pair_rows(c * tile_rows + r), slot * pixels:(slot + 1) * pixels] = joined(
                        near_block(r, c, slot), near_block(r + 1, c, slot))
            return carry

        lax.fori_loop(0, tile_cols, gather, 0)
        product = lax.dot_general(
            near_g[...], near_w[sub, :, base * pixels:(base + part_slots) * pixels], contract,
            preferred_element_type=jnp.float32)
        if part == 0:
            near_acc[...] = product
        else:
            near_acc[...] += product

    def far_group(blocks, col0, size, targets):
        rows = size * tile_rows * half
        depth = far_slots * pixels

        def body(c, carry):
            for who, (tile, _) in enumerate(targets):
                def far_block(r, sub, slot):
                    return blocks[far_codes_s[tile, sub, r, slot, col0 + c], c]

                for r in range(0, tile_rows, 2):
                    for sub in range(2):
                        for slot in range(far_slots):
                            at = sub * far_slots + slot
                            far_g[pair_rows((who * size + c) * tile_rows + r), at * pixels:(at + 1) * pixels] = joined(
                                far_block(r, sub, slot), far_block(r + 1, sub, slot))
            return carry

        lax.fori_loop(0, size, body, 0)
        total = len(targets) * rows
        product = lax.dot_general(
            far_g[:total, :depth], far_w[0], contract, preferred_element_type=jnp.float32)
        product += lax.dot_general(
            far_g[:total, depth:], far_w[1], contract, preferred_element_type=jnp.float32)
        far_acc[:total, :] = product

        def subtract(c, carry):
            for who, (tile, put) in enumerate(targets):
                for r in range(tile_rows):
                    value = blocks[tile * tile_rows + r, c].astype(jnp.float32)
                    put(r, c, value - far_acc[block_rows((who * size + c) * tile_rows + r), :])
            return carry

        lax.fori_loop(0, size, subtract, 0)

    def fine(r, c):
        return near[edge + r, edge + c].astype(jnp.float32) - near_acc[block_rows(c * tile_rows + r), :]

    def put_own(col0):
        def put(r, c, white):
            white_own[r, col0 + c] = white.astype(jnp.bfloat16)
        return put

    def put_served(which):
        def put(r, c, white):
            white_served[which, r, c] = white.astype(jnp.bfloat16)
        return put

    def put_both(col0):
        def put(r, c, white):
            white_both[r, col0 - starts[0] + c] = white.astype(jnp.bfloat16)
        return put

    def finish(first, last, whites):
        def body(c, carry):
            for r in range(tile_rows):
                white = whites[r, c].astype(jnp.float32)
                out[r, c] = jnp.where(levels_s[r, c] == 1, fine(r, c), white).astype(jnp.bfloat16)
            return carry

        lax.fori_loop(first, last, body, 0)

    def far_late(k):
        mid_rest[k - 1].wait_recv()
        relay_both[k].wait_recv()
        late_edges[k - 1].wait()
        far_group(far_both[k], starts[k], sizes[k], [(end, put_both(starts[k])), (i, put_own(starts[k]))])
        white_end_both[k].start()

    @pl.when(is_mid)
    def _():
        mid_theirs.wait_recv()
        end_served.wait_recv()
        relay_theirs.wait_recv()
        end_halos[1].start()
        mid_halos[0].start()
        far_group(far_served, served_at, served, [
            (far_end, put_served(2)), (far_mid, put_served(1)), (end, put_served(0)), (i, put_own(served_at))])
        white_end.start()
        mid_first.wait_recv()
        relay_both[0].wait_recv()
        mid_halos[1].start()
        far_group(far_both[0], starts[0], sizes[0], [(end, put_both(starts[0])), (i, put_own(starts[0]))])
        white_end_both[0].start()
        for k in range(1, chunks):
            end_both[k].wait_recv()
            relay_both[k].start()
            end_halos[2 + k].start()
        white_far_end.start()
        white_far_mid.start()
        edge_served.wait_recv()
        edge_late.wait_recv()
        for copy in late_edges:
            copy.start()
        for copy in end_halos + mid_halos:
            copy.wait()
        near_part(0)
        near_part(1)
        for k in range(1, chunks):
            far_late(k)
        near_part(2)
        near_part(3)
        finish(served_at, served_at + served, white_own)
        finish(starts[0], tile_cols, white_own)
        white_far_mid.wait_recv()
        finish(theirs_at, theirs_at + served, white_in)

    @pl.when(is_end)
    def _():
        back_edge.wait_recv()
        for part in range(PARTS):
            near_part(part)
        white_end.wait_recv()
        finish(served_at, served_at + served, white_in)
        for k in range(chunks - 1):
            white_end_both[k].wait_recv()
            finish(starts[k], starts[k + 1], white_in)
        white_far_end.wait_recv()
        finish(theirs_at, theirs_at + served, white_in)
        white_end_both[chunks - 1].wait_recv()
        finish(starts[chunks - 1], starts[chunks], white_in)

    for flow in small + large + sides + factors + [code_relay] + code_share:
        flow.wait_send()
    for flow in [relay_theirs, edge_served, edge_late] + relay_both + mid_rest:
        flow.wait_send()
    for d in diagonals:
        corners[d].wait_send()
    for flow in [white_far_end, white_far_mid, white_end] + white_end_both:
        flow.wait_send()


def put_out(src, dst, sem):
    pieces = sem.shape[0]
    size = src.shape[0] // pieces
    copies = [
        pltpu.make_async_copy(src.at[pl.ds(k * size, size)], dst.at[pl.ds(k * size, size)], sem.at[k])
        for k in range(pieces)
    ]
    for copy in copies:
        copy.start()
    for copy in copies:
        copy.wait()


def pair_on_device(convergence, block_level, near_codes, far_rows, near_factor, far_factor):
    tile_rows, tile_cols, samples, pixels = convergence.shape
    n_rows, n_cols = lax.axis_size("rows"), lax.axis_size("cols")
    near_slots, far_slots = near_codes.shape[2], far_rows.shape[2]
    half = samples // 2
    served = tile_cols // 4
    starts = group_starts(tile_cols, served)
    sizes = [starts[k + 1] - starts[k] for k in range(len(starts) - 1)]
    near_codes = jnp.transpose(near_codes, (0, 2, 1))
    far_codes = jnp.transpose(far_rows, (0, 2, 1))
    dims = (n_rows, n_cols, tile_rows, tile_cols, half, pixels, near_slots, far_slots, served)
    block = (half, pixels)
    bf16, f32, i32 = jnp.bfloat16, jnp.float32, jnp.int32
    all_rows = tile_rows * tile_cols * half
    group_rows = tile_rows * half * max([n_rows * served] + [2 * size for size in sizes])
    dma = pltpu.SemaphoreType.DMA
    scratch = [pltpu.VMEM((n_rows * tile_rows, size) + block, bf16) for size in sizes]
    scratch += [
        pltpu.VMEM((n_rows * tile_rows, served) + block, bf16),
        pltpu.VMEM((tile_rows + 4, tile_cols + 4) + block, bf16),
        pltpu.VMEM((tile_rows, served) + block, bf16),
        pltpu.VMEM((4, 2, 2) + block, bf16),
        pltpu.VMEM((2,) + near_factor.shape, bf16),
        pltpu.VMEM((2,) + far_factor.shape, bf16),
        pltpu.VMEM((2,) + near_codes.shape, i32),
        pltpu.VMEM((n_rows, 2) + far_codes.shape, i32),
        pltpu.SMEM((2,) + near_codes.shape, i32),
        pltpu.SMEM((n_rows, 2) + far_codes.shape, i32),
        pltpu.SMEM(block_level.shape, i32),
        pltpu.VMEM((all_rows, 2 * near_slots // PARTS * pixels), bf16),
        pltpu.VMEM((group_rows, 2 * far_slots * pixels), bf16),
        pltpu.VMEM((all_rows, pixels), f32),
        pltpu.VMEM((group_rows, pixels), f32),
        pltpu.VMEM((3, tile_rows, served) + block, bf16),
        pltpu.VMEM((tile_rows, tile_cols - 2 * served) + block, bf16),
        pltpu.VMEM((tile_rows, tile_cols) + block, bf16),
        pltpu.VMEM((tile_rows, tile_cols) + block, bf16),
        dma((30 + 4 * len(sizes),)),
        dma((30 + 4 * len(sizes),)),
        dma((16 + 3 * len(sizes),)),
    ]
    anywhere = pl.BlockSpec(memory_space=pl.ANY)
    vmem = pl.BlockSpec(memory_space=pltpu.VMEM)
    white = pl.pallas_call(
        functools.partial(pair_kernel, dims),
        out_shape=pltpu.VMEM((tile_rows, tile_cols) + block, bf16),
        in_specs=[anywhere] * 6,
        out_specs=vmem,
        scratch_shapes=scratch,
        compiler_params=pltpu.CompilerParams(
            collective_id=0, has_side_effects=True, vmem_limit_bytes=56 * 1024 * 1024),
    )(convergence, near_codes, far_codes, block_level, near_factor, far_factor)
    return pl.pallas_call(
        put_out,
        out_shape=jax.ShapeDtypeStruct(white.shape, bf16),
        in_specs=[vmem],
        out_specs=anywhere,
        scratch_shapes=[dma((tile_rows,))],
    )(pltpu.with_memory_space_constraint(white, pltpu.VMEM))


def solution(mesh):
    placed = (
        P(("fields", "rows"), "cols", None, None),
        P(("fields", "rows"), "cols"),
        P(("fields", "rows"), "cols", "sub"),
        P(("fields", "rows"), "cols", "sub"),
        P(None, "sub"),
        P(None, "sub"),
    )
    two_middle_tiles = mesh.shape["rows"] - 2 == 2
    return jax.shard_map(
        pair_on_device if two_middle_tiles else on_device,
        mesh=mesh,
        in_specs=placed,
        out_specs=P(("fields", "rows"), "cols", "sub", None),
        check_vma=False,
    )
```

```python
import functools

import jax
import jax.numpy as jnp
from jax import lax
from jax.experimental import pallas as pl
from jax.experimental.pallas import tpu as pltpu
from jax.sharding import PartitionSpec as P

MESH = pl.DeviceIdType.MESH
PARTS = 4


def chunk_starts(cols):
    return [0, cols * 5 // 16, cols * 10 // 16, cols * 14 // 16, cols]


def kernel(dims, conv, codes, near_factor, far_factor, out, *scratch):
    n_rows, n_cols, tile_rows, tile_cols, half, pixels, near_slots, far_slots = dims
    starts = chunk_starts(tile_cols)
    chunks = len(starts) - 1
    sizes = [starts[k + 1] - starts[k] for k in range(chunks)]
    far = scratch[:chunks]
    (near, near_w, far_w, codes_v, codes_s, near_g, far_g, near_acc, far_acc, end_acc,
     white_src, white_dst, tile_send, tile_recv, white_send, white_recv,
     side_send, side_recv, corner_send, corner_recv, code_send, code_recv, fac_send, fac_recv, loc_sem, halo_sem) = scratch[chunks:]

    i = lax.axis_index("rows")
    x = lax.axis_index("cols")
    s = lax.axis_index("sub")
    other = 1 - s
    mine = pl.ds(pl.multiple_of(s * half, half), half)
    is_end = (i == 0) | (i == n_rows - 1)
    is_mid = (i > 0) & (i < n_rows - 1)
    low_helper = i == 1
    high_helper = i == n_rows - 2
    is_helper = low_helper | high_helper
    end_tile = jnp.where(low_helper, 0, n_rows - 1)
    to_mid = jnp.where(i == 0, 1, n_rows - 2)

    def cols_of(k):
        return pl.ds(starts[k], sizes[k])

    local = [
        pltpu.make_async_copy(
            conv.at[:, :, mine, :],
            near.at[pl.ds(2, tile_rows), pl.ds(2, tile_cols)],
            loc_sem.at[0],
        ),
        pltpu.make_async_copy(near_factor, near_w.at[s], loc_sem.at[1]),
        pltpu.make_async_copy(far_factor, far_w.at[s], loc_sem.at[2]),
        pltpu.make_async_copy(codes, codes_s.at[0, s], loc_sem.at[3]),
    ]
    for copy in local:
        copy.start()
    own_far = [
        pltpu.make_async_copy(
            conv.at[:, cols_of(k), mine, :],
            far[k].at[pl.ds(i * tile_rows, tile_rows)],
            loc_sem.at[6 + k],
        )
        for k in range(chunks)
    ]

    @pl.when(is_mid)
    def _():
        for copy in own_far:
            copy.start()

    @pl.when(i == 0)
    def _():
        near[0:2] = jnp.zeros((2,) + near.shape[1:], near.dtype)

    @pl.when(i == n_rows - 1)
    def _():
        near[tile_rows + 2:tile_rows + 4] = jnp.zeros((2,) + near.shape[1:], near.dtype)

    @pl.when(x == 0)
    def _():
        near[:, 0:2] = jnp.zeros((near.shape[0], 2) + near.shape[2:], near.dtype)

    @pl.when(x == n_cols - 1)
    def _():
        near[:, tile_cols + 2:tile_cols + 4] = jnp.zeros((near.shape[0], 2) + near.shape[2:], near.dtype)

    barrier = pltpu.get_barrier_semaphore()
    offsets = [(-1, 0), (1, 0), (0, -1), (0, 1)]

    def present(di, dx):
        ok = jnp.bool_(True)
        if di == -1:
            ok = ok & (i > 0)
        if di == 1:
            ok = ok & (i < n_rows - 1)
        if dx == -1:
            ok = ok & (x > 0)
        if dx == 1:
            ok = ok & (x < n_cols - 1)
        return ok

    for di, dx in offsets:
        @pl.when(present(di, dx))
        def _():
            pl.semaphore_signal(barrier, inc=1, device_id={"rows": i + di, "cols": x + dx}, device_id_type=MESH)
    pl.semaphore_signal(barrier, inc=1, device_id={"sub": other}, device_id_type=MESH)
    count_z = (i > 0).astype(jnp.int32) + (i < n_rows - 1).astype(jnp.int32)
    count_x = (x > 0).astype(jnp.int32) + (x < n_cols - 1).astype(jnp.int32)
    pl.semaphore_wait(barrier, count_z + count_x + 1)

    def code_copy(which, slot, target):
        return pltpu.make_async_remote_copy(
            src_ref=codes if which < 2 else codes_v.at[slot, s], dst_ref=codes_v.at[slot, s],
            send_sem=code_send.at[which], recv_sem=code_recv.at[which], device_id=target, device_id_type=MESH)

    code_partner = code_copy(0, 0, {"sub": other})
    code_straight = code_copy(1, 1, {"rows": to_mid})
    code_relay = code_copy(2, 1, {"sub": other})
    code_partner.start()

    @pl.when(is_end)
    def _():
        code_straight.start()

    def side_copy(di, dx):
        if di == 0:
            rows_src, rows_dst = pl.ds(0, tile_rows), pl.ds(2, tile_rows)
        elif di == -1:
            rows_src, rows_dst = pl.ds(0, 2), pl.ds(tile_rows + 2, 2)
        else:
            rows_src, rows_dst = pl.ds(tile_rows - 2, 2), pl.ds(0, 2)
        if dx == 0:
            cols_src, cols_dst = pl.ds(0, tile_cols), pl.ds(2, tile_cols)
        elif dx == -1:
            cols_src, cols_dst = pl.ds(0, 2), pl.ds(tile_cols + 2, 2)
        else:
            cols_src, cols_dst = pl.ds(tile_cols - 2, 2), pl.ds(0, 2)
        which = offsets.index((di, dx))
        return pltpu.make_async_remote_copy(
            src_ref=conv.at[rows_src, cols_src, mine, :],
            dst_ref=near.at[rows_dst, cols_dst],
            send_sem=side_send.at[which], recv_sem=side_recv.at[which],
            device_id={"rows": i + di, "cols": x + dx}, device_id_type=MESH)

    def side_sends(di, dx):
        if dx == 0:
            return low_helper if di == -1 else high_helper
        return present(di, dx)

    def side_receives(di, dx):
        if dx == 0:
            return (i == 0) if di == -1 else (i == n_rows - 1)
        return present(-di, -dx)

    def tile_copy(way, d, k, tile):
        src = conv.at[:, cols_of(k), mine, :] if d == 0 else far[k].at[pl.ds(tile * tile_rows, tile_rows)]
        return pltpu.make_async_remote_copy(
            src_ref=src, dst_ref=far[k].at[pl.ds(tile * tile_rows, tile_rows)],
            send_sem=tile_send.at[way, d, k], recv_sem=tile_recv.at[way, d, k],
            device_id={"rows": i - 1 if way == 0 else i + 1}, device_id_type=MESH)

    def sent(way, d, k):
        return tile_copy(way, d, k, i + d if way == 0 else i - d)

    def received(way, d, k):
        return tile_copy(way, d, k, i + 1 + d if way == 0 else i - 1 - d)

    def tile_sends(way, d):
        if way == 0:
            return (i >= 2) & (i + d <= n_rows - 1)
        return (i <= n_rows - 3) & (i - d >= 0)

    def tile_receives(way, d):
        if way == 0:
            return is_mid & (i + 1 + d <= n_rows - 1)
        return is_mid & (i - 1 - d >= 0)

    for k in range(chunks):
        for way in (0, 1):
            @pl.when(tile_sends(way, 0))
            def _():
                sent(way, 0, k).start()
        if k == 0:
            for di, dx in offsets:
                @pl.when(side_sends(di, dx))
                def _():
                    side_copy(di, dx).start()

    def factor_copy(which):
        src, dst = ((near_factor, near_w), (far_factor, far_w))[which]
        return pltpu.make_async_remote_copy(
            src_ref=src, dst_ref=dst.at[s], send_sem=fac_send.at[which],
            recv_sem=fac_recv.at[which], device_id={"sub": other}, device_id_type=MESH)

    for which in (0, 1):
        factor_copy(which).start()

    def halo_copy(way, k):
        if way == 0:
            src_rows, dst_rows = pl.ds((i + 1) * tile_rows, 2), pl.ds(tile_rows + 2, 2)
        else:
            src_rows, dst_rows = pl.ds(i * tile_rows - 2, 2), pl.ds(0, 2)
        return pltpu.make_async_copy(
            far[k].at[src_rows], near.at[dst_rows, pl.ds(2 + starts[k], sizes[k])], halo_sem.at[way, k])

    for d in range(n_rows - 3):
        for k in range(chunks):
            for way in (0, 1):
                @pl.when(tile_receives(way, d))
                def _():
                    received(way, d, k).wait_recv()
                    if d == 0:
                        halo_copy(way, k).start()

                @pl.when(tile_sends(way, d + 1))
                def _():
                    sent(way, d + 1, k).start()

    code_copy(0, 0, {"sub": other}).wait_recv()
    code_in = pltpu.make_async_copy(codes_v.at[0, other], codes_s.at[0, other], loc_sem.at[4])
    code_in.start()
    end_codes = pltpu.make_async_copy(codes_v.at[1], codes_s.at[1], loc_sem.at[5])

    @pl.when(is_helper)
    def _():
        code_straight.wait_recv()
        code_relay.start()

    for copy in local:
        copy.wait()

    @pl.when(is_mid)
    def _():
        for k in range(chunks):
            halo_copy(0, k).wait()
            halo_copy(1, k).wait()
            own_far[k].wait()

    for di, dx in offsets:
        @pl.when(side_receives(di, dx))
        def _():
            side_copy(di, dx).wait_recv()

    def corner_copy(di, dx):
        rows = pl.ds(0, 2) if di == -1 else pl.ds(tile_rows + 2, 2)
        src, dst = (2, tile_cols + 2) if dx == -1 else (tile_cols, 0)
        which = (di + 1) + (dx + 1) // 2
        return pltpu.make_async_remote_copy(
            src_ref=near.at[rows, pl.ds(src, 2)], dst_ref=near.at[rows, pl.ds(dst, 2)],
            send_sem=corner_send.at[which], recv_sem=corner_recv.at[which],
            device_id={"cols": x + dx}, device_id_type=MESH)

    corners = [(di, dx) for di in (-1, 1) for dx in (-1, 1)]
    for di, dx in corners:
        @pl.when(present(di, 0) & present(0, dx))
        def _():
            corner_copy(di, dx).start()

    @pl.when(is_helper)
    def _():
        code_relay.wait_recv()
        end_codes.start()
        end_codes.wait()

    code_in.wait()
    for which in (0, 1):
        factor_copy(which).wait_recv()
    for di, dx in corners:
        @pl.when(present(di, 0) & present(0, -dx))
        def _():
            corner_copy(di, dx).wait_recv()

    contract = (((1,), (1,)), ((), ()))
    part_slots = 2 * near_slots // PARTS

    def block_rows(block):
        return pl.ds(pl.multiple_of(block * half, half), half)

    def pair_rows(block):
        return pl.ds(pl.multiple_of(block * half, 2 * half), 2 * half)

    def joined(first, second):
        both = jnp.concatenate([first.astype(jnp.float32), second.astype(jnp.float32)], axis=0)
        return both.astype(jnp.bfloat16)

    def near_part(part):
        sub, base = part * part_slots // near_slots, part * part_slots % near_slots

        def near_block(r, c, slot):
            code = codes_s[0, sub, r, base + slot, c]
            down = lax.shift_right_logical(code * 205, 10)
            return near[r + down, c + code - 5 * down]

        def gather(c, carry):
            for r in range(0, tile_rows, 2):
                for slot in range(part_slots):
                    near_g[pair_rows(c * tile_rows + r), slot * pixels:(slot + 1) * pixels] = joined(
                        near_block(r, c, slot), near_block(r + 1, c, slot))
            return carry

        lax.fori_loop(0, tile_cols, gather, 0)
        product = lax.dot_general(
            near_g[...], near_w[sub, :, base * pixels:(base + part_slots) * pixels], contract,
            preferred_element_type=jnp.float32)
        if part == 0:
            near_acc[...] = product
        else:
            near_acc[...] += product

    level_at = near_slots + far_slots

    def far_chunk(k):
        rows = sizes[k] * tile_rows * half

        def gather_far(who):
            def far_block(r, c, sub, slot):
                row = codes_s[who, sub, r, near_slots + slot, starts[k] + c]
                return far[k][row, c]

            def body(c, carry):
                for r in range(0, tile_rows, 2):
                    for sub in range(2):
                        for slot in range(far_slots):
                            at = sub * far_slots + slot
                            far_g[pair_rows((who * sizes[k] + c) * tile_rows + r), at * pixels:(at + 1) * pixels] = joined(
                                far_block(r, c, sub, slot), far_block(r + 1, c, sub, slot))
                return carry

            lax.fori_loop(0, sizes[k], body, 0)

        gather_far(0)

        @pl.when(is_helper)
        def _():
            gather_far(1)

        depth = far_slots * pixels
        product = lax.dot_general(
            far_g[:2 * rows, :depth], far_w[0], contract, preferred_element_type=jnp.float32)
        product += lax.dot_general(
            far_g[:2 * rows, depth:], far_w[1], contract, preferred_element_type=jnp.float32)
        far_acc[pl.ds(starts[k] * tile_rows * half, rows), :] = product[:rows]
        end_acc[pl.ds(0, rows), :] = product[rows:]

        @pl.when(is_helper)
        def _():
            def body(c, carry):
                for r in range(tile_rows):
                    value = far[k][end_tile * tile_rows + r, c].astype(jnp.float32)
                    white_src[r, starts[k] + c] = (value - end_acc[block_rows(c * tile_rows + r), :]).astype(jnp.bfloat16)
                return carry

            lax.fori_loop(0, sizes[k], body, 0)
            white_copy(k).start()

    def white_copy(k):
        return pltpu.make_async_remote_copy(
            src_ref=white_src.at[:, cols_of(k)], dst_ref=white_dst.at[:, cols_of(k)],
            send_sem=white_send.at[k], recv_sem=white_recv.at[k],
            device_id={"rows": end_tile}, device_id_type=MESH)

    @pl.when(is_mid)
    def _():
        near_part(0)
        for k in range(chunks):
            d = n_rows - 3
            for way in (0, 1):
                @pl.when(tile_receives(way, d))
                def _():
                    received(way, d, k).wait_recv()
            far_chunk(k)
            if k < PARTS - 2:
                near_part(k + 1)
        near_part(PARTS - 1)

        def body(c, carry):
            for r in range(tile_rows):
                level = codes_s[0, s, r, level_at, c]
                at = block_rows(c * tile_rows + r)
                mean = jnp.where(level == 1, near_acc[at, :], far_acc[at, :])
                out[r, c] = (near[2 + r, 2 + c].astype(jnp.float32) - mean).astype(jnp.bfloat16)
            return carry

        lax.fori_loop(0, tile_cols, body, 0)

    @pl.when(is_end)
    def _():
        for part in range(PARTS):
            near_part(part)
        for k in range(chunks):
            white_copy(k).wait_recv()

            def body(c, carry):
                for r in range(tile_rows):
                    level = codes_s[0, s, r, level_at, c]
                    mean = near_acc[block_rows(c * tile_rows + r), :]
                    fine = near[2 + r, 2 + c].astype(jnp.float32) - mean
                    coarse = white_dst[r, c].astype(jnp.float32)
                    out[r, c] = jnp.where(level == 1, fine, coarse).astype(jnp.bfloat16)
                return carry

            lax.fori_loop(starts[k], starts[k + 1], body, 0)

    code_partner.wait_send()

    @pl.when(is_end)
    def _():
        code_straight.wait_send()

    for di, dx in corners:
        @pl.when(present(di, 0) & present(0, dx))
        def _():
            corner_copy(di, dx).wait_send()

    for di, dx in offsets:
        @pl.when(side_sends(di, dx))
        def _():
            side_copy(di, dx).wait_send()
    for which in (0, 1):
        factor_copy(which).wait_send()
    for d in range(n_rows - 2):
        for way in (0, 1):
            @pl.when(tile_sends(way, d))
            def _():
                for k in range(chunks):
                    sent(way, d, k).wait_send()

    @pl.when(is_helper)
    def _():
        code_relay.wait_send()
        for k in range(chunks):
            white_copy(k).wait_send()


def on_device(convergence, block_level, near_codes, far_rows, near_factor, far_factor):
    tile_rows, tile_cols, samples, pixels = convergence.shape
    n_rows, n_cols = lax.axis_size("rows"), lax.axis_size("cols")
    near_slots, far_slots = near_codes.shape[2], far_rows.shape[2]
    half = samples // 2
    starts = chunk_starts(tile_cols)
    chunks = len(starts) - 1
    codes = jnp.concatenate(
        [jnp.transpose(near_codes, (0, 2, 1)), jnp.transpose(far_rows, (0, 2, 1)), block_level[:, None, :]], axis=1)
    dims = (n_rows, n_cols, tile_rows, tile_cols, half, pixels, near_slots, far_slots)
    block = (half, pixels)
    bf16, f32 = jnp.bfloat16, jnp.float32
    all_rows = tile_rows * tile_cols * half
    chunk_rows = tile_rows * half * max(starts[k + 1] - starts[k] for k in range(chunks))
    dma = pltpu.SemaphoreType.DMA
    scratch = [pltpu.VMEM((n_rows * tile_rows, starts[k + 1] - starts[k]) + block, bf16) for k in range(chunks)]
    scratch += [
        pltpu.VMEM((tile_rows + 4, tile_cols + 4) + block, bf16),
        pltpu.VMEM((2,) + near_factor.shape, bf16),
        pltpu.VMEM((2,) + far_factor.shape, bf16),
        pltpu.VMEM((2, 2) + codes.shape, jnp.int32),
        pltpu.SMEM((2, 2) + codes.shape, jnp.int32),
        pltpu.VMEM((all_rows, 2 * near_slots // PARTS * pixels), bf16),
        pltpu.VMEM((2 * chunk_rows, 2 * far_slots * pixels), bf16),
        pltpu.VMEM((all_rows, pixels), f32),
        pltpu.VMEM((all_rows, pixels), f32),
        pltpu.VMEM((chunk_rows, pixels), f32),
        pltpu.VMEM((tile_rows, tile_cols) + block, bf16),
        pltpu.VMEM((tile_rows, tile_cols) + block, bf16),
        dma((2, n_rows - 2, chunks)),
        dma((2, n_rows - 2, chunks)),
        dma((chunks,)),
        dma((chunks,)),
        dma((4,)),
        dma((4,)),
        dma((4,)),
        dma((4,)),
        dma((3,)),
        dma((3,)),
        dma((2,)),
        dma((2,)),
        dma((6 + chunks,)),
        dma((2, chunks)),
    ]
    anywhere = pl.BlockSpec(memory_space=pl.ANY)
    vmem = pl.BlockSpec(memory_space=pltpu.VMEM)
    return pl.pallas_call(
        functools.partial(kernel, dims),
        out_shape=jax.ShapeDtypeStruct((tile_rows, tile_cols) + block, bf16),
        in_specs=[anywhere, vmem, anywhere, anywhere],
        out_specs=vmem,
        scratch_shapes=scratch,
        compiler_params=pltpu.CompilerParams(
            collective_id=0, has_side_effects=True, vmem_limit_bytes=56 * 1024 * 1024),
    )(convergence, codes, near_factor, far_factor)


def group_starts(cols, served):
    left = cols - 2 * served
    return [2 * served, 2 * served + left // 2, 2 * served + left * 3 // 4, cols]


def pair_kernel(dims, conv, near_codes, far_codes, levels, near_factor, far_factor, out, *scratch):
    n_rows, n_cols, tile_rows, tile_cols, half, pixels, near_slots, far_slots, served = dims
    starts = group_starts(tile_cols, served)
    chunks = len(starts) - 1
    sizes = [starts[k + 1] - starts[k] for k in range(chunks)]
    far_both = scratch[:chunks]
    (far_served, near, stage, bits, near_w, far_w, near_codes_v, far_codes_v, near_codes_s, far_codes_s, levels_s,
     near_g, far_g, near_acc, far_acc, white_served, white_both, white_own, white_in, send_sem, recv_sem, loc_sem) = scratch[chunks:]

    i = lax.axis_index("rows")
    x = lax.axis_index("cols")
    s = lax.axis_index("sub")
    other = 1 - s
    mine = pl.ds(pl.multiple_of(s * half, half), half)
    low = i < n_rows // 2
    mid = jnp.where(low, n_rows // 2 - 1, n_rows // 2)
    end = jnp.where(low, 0, n_rows - 1)
    far_mid, far_end = n_rows - 1 - mid, n_rows - 1 - end
    is_mid = i == mid
    is_end = i == end
    always = i >= 0
    edge = 2
    rest = tile_rows - edge
    in_edge = jnp.where(low, tile_rows - edge, 0)
    in_rest = jnp.where(low, 0, edge)
    out_edge = jnp.where(low, 0, tile_rows - edge)
    below, above = 0, tile_rows + edge
    served_at = jnp.where(low, 0, served)
    theirs_at = served - served_at
    served_cols, theirs_cols = pl.ds(served_at, served), pl.ds(theirs_at, served)
    inner = pl.ds(edge, tile_cols)
    count = {"remote": 0, "local": 0}

    class Remote:
        def __init__(self, sends, receives, src, dst, landed, to):
            self.at, self.sends, self.receives = count["remote"], sends, receives
            self.src, self.dst, self.landed, self.to = src, dst, landed, to
            count["remote"] += 1

        def copy(self, src, dst):
            return pltpu.make_async_remote_copy(
                src_ref=src, dst_ref=dst, send_sem=send_sem.at[self.at], recv_sem=recv_sem.at[self.at],
                device_id=self.to, device_id_type=MESH)

        def start(self):
            @pl.when(self.sends)
            def _():
                self.copy(self.src, self.dst).start()

        def wait_recv(self):
            @pl.when(self.receives)
            def _():
                self.copy(self.landed, self.landed).wait_recv()

        def wait_send(self):
            @pl.when(self.sends)
            def _():
                self.copy(self.src, self.dst).wait_send()

    class Local:
        def __init__(self, here, src, dst):
            self.here = here
            self.copy = pltpu.make_async_copy(src, dst, loc_sem.at[count["local"]])
            count["local"] += 1

        def start(self):
            @pl.when(self.here)
            def _():
                self.copy.start()

        def wait(self):
            @pl.when(self.here)
            def _():
                self.copy.wait()

    def rows_of(tile, first, size):
        return pl.ds(tile * tile_rows + first, size)

    def both_cols(k):
        return pl.ds(starts[k], sizes[k])

    to_partner, to_mid, to_end = {"sub": other}, {"rows": mid}, {"rows": end}
    to_far_mid, to_far_end = {"rows": far_mid}, {"rows": far_end}

    own = [
        Local(always, conv.at[:, :, mine, :], near.at[pl.ds(edge, tile_rows), inner]),
        Local(always, near_factor, near_w.at[s]),
        Local(is_mid, far_factor, far_w.at[s]),
        Local(always, near_codes, near_codes_s.at[s]),
        Local(always, levels, levels_s),
        Local(is_mid, far_codes, far_codes_s.at[i, s]),
        Local(is_mid, conv.at[:, served_cols, mine, :], far_served.at[rows_of(i, 0, tile_rows)]),
    ] + [
        Local(is_mid, conv.at[:, both_cols(k), mine, :], far_both[k].at[rows_of(i, 0, tile_rows)])
        for k in range(chunks)
    ]
    for copy in own:
        copy.start()

    def clear(where, rows, cols):
        @pl.when(where)
        def _():
            near[rows, cols] = jnp.zeros((rows.stop - rows.start, cols.stop - cols.start) + near.shape[2:], near.dtype)

    clear(i == 0, slice(0, edge), slice(0, tile_cols + 2 * edge))
    clear(i == n_rows - 1, slice(above, above + edge), slice(0, tile_cols + 2 * edge))
    clear(x == 0, slice(0, tile_rows + 2 * edge), slice(0, edge))
    clear(x == n_cols - 1, slice(0, tile_rows + 2 * edge), slice(tile_cols + edge, tile_cols + 2 * edge))

    def present(di, dx):
        ok = always
        if di == -1:
            ok = ok & (i > 0)
        if di == 1:
            ok = ok & (i < n_rows - 1)
        if dx == -1:
            ok = ok & (x > 0)
        if dx == 1:
            ok = ok & (x < n_cols - 1)
        return ok

    barrier = pltpu.get_barrier_semaphore()
    for di, dx in ((-1, 0), (1, 0), (0, -1), (0, 1)):
        @pl.when(present(di, dx))
        def _():
            pl.semaphore_signal(barrier, inc=1, device_id={"rows": i + di, "cols": x + dx}, device_id_type=MESH)
    pl.semaphore_signal(barrier, inc=1, device_id=to_partner, device_id_type=MESH)
    count_z = (i > 0).astype(jnp.int32) + (i < n_rows - 1).astype(jnp.int32)
    count_x = (x > 0).astype(jnp.int32) + (x < n_cols - 1).astype(jnp.int32)
    pl.semaphore_wait(barrier, count_z + count_x + 1)

    def exchange(src, dst, landed):
        return Remote(always, always, src, dst, landed, to_partner)

    def inward(src, dst, landed):
        return Remote(is_end, is_mid, src, dst, landed, to_mid)

    def outward(src, dst, landed):
        return Remote(is_mid, is_end, src, dst, landed, to_end)

    def across(src, dst, landed):
        return Remote(is_mid, is_mid, src, dst, landed, to_far_mid)

    def between(src, dst, landed):
        return Remote(is_mid, is_mid, src, dst, landed, to_partner)

    from_inside = pl.ds(jnp.where(low, above, below), edge)
    from_outside = pl.ds(jnp.where(low, below, above), edge)
    late_cols = pl.ds(starts[1], tile_cols - starts[1])

    code_near = exchange(near_codes, near_codes_v.at[s], near_codes_v.at[other])
    code_own = between(far_codes, far_codes_v.at[i, s], far_codes_v.at[i, other])
    code_end = inward(far_codes, far_codes_v.at[end, s], far_codes_v.at[end, s])
    code_mid = across(far_codes, far_codes_v.at[mid, s], far_codes_v.at[far_mid, s])
    code_relay = across(far_codes_v.at[end, s], far_codes_v.at[end, s], far_codes_v.at[far_end, s])
    code_share = [
        between(far_codes_v.at[tile, s], far_codes_v.at[tile, s], far_codes_v.at[tile, other])
        for tile in (end, far_mid, far_end)
    ]

    def halo(rows, first, size):
        return near.at[rows, pl.ds(edge + first, size)]

    def in_edge_of(cols):
        return conv.at[pl.ds(in_edge, edge), cols, mine, :]

    def all_rows_of(cols):
        return conv.at[:, cols, mine, :]

    def tile_of(ref, tile):
        return ref.at[rows_of(tile, 0, tile_rows)]

    back_edge = outward(
        conv.at[pl.ds(out_edge, edge), :, mine, :], near.at[from_inside, inner], near.at[from_inside, inner])
    mid_theirs = across(all_rows_of(theirs_cols), tile_of(far_served, mid), tile_of(far_served, far_mid))
    mid_first = across(all_rows_of(both_cols(0)), tile_of(far_both[0], mid), tile_of(far_both[0], far_mid))
    edge_served = across(
        in_edge_of(served_cols), halo(from_outside, served_at, served), halo(from_inside, theirs_at, served))
    edge_late = across(
        in_edge_of(late_cols), halo(from_outside, late_cols.start, late_cols.size),
        halo(from_inside, late_cols.start, late_cols.size))
    their_rest = jnp.where(low, edge, 0)
    mid_rest = [
        across(
            conv.at[pl.ds(in_rest, rest), both_cols(k), mine, :], far_both[k].at[rows_of(mid, in_rest, rest)],
            far_both[k].at[rows_of(far_mid, their_rest, rest)])
        for k in range(1, chunks)
    ]

    def end_to(cols, ref):
        return inward(all_rows_of(cols), ref, ref)

    end_theirs = end_to(theirs_cols, stage)
    end_served = end_to(served_cols, tile_of(far_served, end))
    end_both = [end_to(both_cols(k), tile_of(far_both[k], end)) for k in range(chunks)]
    relay_theirs = across(stage, tile_of(far_served, end), tile_of(far_served, far_end))
    relay_both = [
        across(tile_of(far_both[k], end), tile_of(far_both[k], end), tile_of(far_both[k], far_end))
        for k in range(chunks)
    ]

    white_far_end = Remote(
        is_mid, is_end, white_served.at[2], white_in.at[:, served_cols], white_in.at[:, theirs_cols], to_far_end)
    white_far_mid = across(white_served.at[1], white_in.at[:, served_cols], white_in.at[:, theirs_cols])
    white_end = outward(white_served.at[0], white_in.at[:, served_cols], white_in.at[:, served_cols])
    white_end_both = [
        outward(
            white_both.at[:, pl.ds(starts[k] - starts[0], sizes[k])], white_in.at[:, both_cols(k)],
            white_in.at[:, both_cols(k)])
        for k in range(chunks)
    ]

    def side_copy(dx):
        src, dst = (0, tile_cols + edge) if dx == -1 else (tile_cols - edge, 0)
        at = near.at[pl.ds(edge, tile_rows), pl.ds(dst, edge)]
        return Remote(
            present(0, dx), present(0, -dx), conv.at[:, pl.ds(src, edge), mine, :], at, at, {"cols": x + dx})

    sides = [side_copy(dx) for dx in (-1, 1)]

    def bit_of(di, dx):
        return bits.at[di + 1 + (dx + 1) // 2]

    def bit_copy(di, dx):
        src = conv.at[
            pl.ds(0 if di == -1 else tile_rows - edge, edge), pl.ds(0 if dx == -1 else tile_cols - edge, edge), mine, :]
        return Remote(
            present(di, 0) & present(0, dx), present(-di, 0) & present(0, dx), src, bit_of(-di, dx), bit_of(-di, dx),
            {"rows": i + di})

    def corner_copy(di, dx):
        at = near.at[pl.ds(below if di == -1 else above, edge), pl.ds(tile_cols + edge if dx == -1 else 0, edge)]
        return Remote(
            present(di, 0) & present(0, dx), present(di, 0) & present(0, -dx), bit_of(di, dx), at, at, {"cols": x + dx})

    diagonals = [(di, dx) for di in (-1, 1) for dx in (-1, 1)]
    bit_flows = {(-di, dx): bit_copy(di, dx) for di, dx in diagonals}
    corners = {(di, dx): corner_copy(di, dx) for di, dx in diagonals}
    factor_near = exchange(near_factor, near_w.at[s], near_w.at[other])
    factor_far = between(far_factor, far_w.at[s], far_w.at[other])

    their_edge = jnp.where(low, 0, tile_rows - edge)
    end_halos = [
        Local(is_mid, stage.at[pl.ds(in_edge, edge)], halo(from_outside, theirs_at, served)),
        Local(is_mid, far_served.at[rows_of(end, in_edge, edge)], halo(from_outside, served_at, served)),
    ] + [
        Local(is_mid, far_both[k].at[rows_of(end, in_edge, edge)], halo(from_outside, starts[k], sizes[k]))
        for k in range(chunks)
    ]
    mid_halos = [
        Local(is_mid, far_served.at[rows_of(far_mid, their_edge, edge)], halo(from_inside, served_at, served)),
        Local(is_mid, far_both[0].at[rows_of(far_mid, their_edge, edge)], halo(from_inside, starts[0], sizes[0])),
    ]
    late_edges = [
        Local(is_mid, halo(from_inside, starts[k], sizes[k]), far_both[k].at[rows_of(far_mid, their_edge, edge)])
        for k in range(1, chunks)
    ]
    near_codes_in = Local(always, near_codes_v.at[other], near_codes_s.at[other])
    far_codes_in = [Local(is_mid, far_codes_v.at[i, other], far_codes_s.at[i, other])] + [
        Local(is_mid, far_codes_v.at[tile], far_codes_s.at[tile]) for tile in (end, far_mid, far_end)
    ]

    small = [code_end, code_mid] + [bit_flows[d] for d in diagonals] + [code_near, code_own]
    large = [mid_theirs, end_theirs, mid_first, end_both[0], back_edge, end_served] + end_both[1:]
    factors = [factor_far, factor_near]
    for flow in small + large + sides + factors:
        flow.start()
    code_end.wait_recv()
    code_relay.start()
    code_share[0].start()
    for d in diagonals:
        bit_flows[d].wait_recv()
        corners[d].start()
    code_mid.wait_recv()
    code_share[1].start()
    code_near.wait_recv()
    near_codes_in.start()
    code_own.wait_recv()
    far_codes_in[0].start()
    for copy in own:
        copy.wait()
    near_codes_in.wait()
    end_theirs.wait_recv()
    relay_theirs.start()
    end_halos[0].start()
    end_both[0].wait_recv()
    relay_both[0].start()
    edge_late.start()
    for flow in mid_rest:
        flow.start()
    end_halos[2].start()
    code_relay.wait_recv()
    code_share[2].start()
    for share in code_share:
        share.wait_recv()
    for copy in far_codes_in[1:]:
        copy.start()
    for copy in far_codes_in:
        copy.wait()
    for factor in factors:
        factor.wait_recv()

    def beside():
        for side in sides:
            side.wait_recv()
        for d in diagonals:
            corners[d].wait_recv()

    contract = (((1,), (1,)), ((), ()))
    part_slots = 2 * near_slots // PARTS

    def block_rows(block):
        return pl.ds(pl.multiple_of(block * half, half), half)

    def pair_rows(block):
        return pl.ds(pl.multiple_of(block * half, 2 * half), 2 * half)

    def joined(first, second):
        both = jnp.concatenate([first.astype(jnp.float32), second.astype(jnp.float32)], axis=0)
        return both.astype(jnp.bfloat16)

    def near_part(part):
        sub, base = part * part_slots // near_slots, part * part_slots % near_slots

        def near_block(r, c, slot):
            code = near_codes_s[sub, r, base + slot, c]
            down = lax.shift_right_logical(code * 205, 10)
            return near[r + down, c + code - 5 * down]

        def gather(c, carry):
            for r in range(0, tile_rows, 2):
                for slot in range(part_slots):
                    near_g[pair_rows(c * tile_rows + r), slot * pixels:(slot + 1) * pixels] = joined(
                        near_block(r, c, slot), near_block(r + 1, c, slot))
            return carry

        lax.fori_loop(0, tile_cols, gather, 0)
        product = lax.dot_general(
            near_g[...], near_w[sub, :, base * pixels:(base + part_slots) * pixels], contract,
            preferred_element_type=jnp.float32)
        if part == 0:
            near_acc[...] = product
        else:
            near_acc[...] += product

    def far_group(blocks, col0, size, targets):
        rows = size * tile_rows * half
        depth = far_slots * pixels

        def body(c, carry):
            for who, (tile, _) in enumerate(targets):
                def far_block(r, sub, slot):
                    return blocks[far_codes_s[tile, sub, r, slot, col0 + c], c]

                for r in range(0, tile_rows, 2):
                    for sub in range(2):
                        for slot in range(far_slots):
                            at = sub * far_slots + slot
                            far_g[pair_rows((who * size + c) * tile_rows + r), at * pixels:(at + 1) * pixels] = joined(
                                far_block(r, sub, slot), far_block(r + 1, sub, slot))
            return carry

        lax.fori_loop(0, size, body, 0)
        total = len(targets) * rows
        product = lax.dot_general(
            far_g[:total, :depth], far_w[0], contract, preferred_element_type=jnp.float32)
        product += lax.dot_general(
            far_g[:total, depth:], far_w[1], contract, preferred_element_type=jnp.float32)
        far_acc[:total, :] = product

        def subtract(c, carry):
            for who, (tile, put) in enumerate(targets):
                for r in range(tile_rows):
                    value = blocks[tile * tile_rows + r, c].astype(jnp.float32)
                    put(r, c, value - far_acc[block_rows((who * size + c) * tile_rows + r), :])
            return carry

        lax.fori_loop(0, size, subtract, 0)

    def fine(r, c):
        return near[edge + r, edge + c].astype(jnp.float32) - near_acc[block_rows(c * tile_rows + r), :]

    def put_own(col0):
        def put(r, c, white):
            white_own[r, col0 + c] = white.astype(jnp.bfloat16)
        return put

    def put_served(which):
        def put(r, c, white):
            white_served[which, r, c] = white.astype(jnp.bfloat16)
        return put

    def put_both(col0):
        def put(r, c, white):
            white_both[r, col0 - starts[0] + c] = white.astype(jnp.bfloat16)
        return put

    def finish(first, last, whites):
        def body(c, carry):
            for r in range(tile_rows):
                white = whites[r, c].astype(jnp.float32)
                out[r, c] = jnp.where(levels_s[r, c] == 1, fine(r, c), white).astype(jnp.bfloat16)
            return carry

        lax.fori_loop(first, last, body, 0)

    def early_sends():
        for flow in small + large + sides + factors + [corners[d] for d in diagonals]:
            flow.wait_send()

    def relay_sends():
        for flow in [code_relay, relay_theirs, edge_served, edge_late] + code_share + relay_both + mid_rest:
            flow.wait_send()

    def far_late(k):
        mid_rest[k - 1].wait_recv()
        relay_both[k].wait_recv()
        late_edges[k - 1].wait()
        far_group(far_both[k], starts[k], sizes[k], [(end, put_both(starts[k])), (i, put_own(starts[k]))])
        white_end_both[k].start()

    @pl.when(is_mid)
    def _():
        mid_theirs.wait_recv()
        end_served.wait_recv()
        relay_theirs.wait_recv()
        end_halos[1].start()
        mid_halos[0].start()
        far_group(far_served, served_at, served, [
            (far_end, put_served(2)), (far_mid, put_served(1)), (end, put_served(0)), (i, put_own(served_at))])
        white_end.start()
        for k in range(1, chunks):
            end_both[k].wait_recv()
            relay_both[k].start()
            end_halos[2 + k].start()
        mid_first.wait_recv()
        relay_both[0].wait_recv()
        mid_halos[1].start()
        far_group(far_both[0], starts[0], sizes[0], [(end, put_both(starts[0])), (i, put_own(starts[0]))])
        white_end_both[0].start()
        edge_served.start()
        white_far_end.start()
        white_far_mid.start()
        edge_late.wait_recv()
        for copy in late_edges:
            copy.start()
        for k in range(1, chunks):
            far_late(k)
        edge_served.wait_recv()
        for copy in end_halos + mid_halos:
            copy.wait()
        beside()
        for part in range(PARTS):
            near_part(part)
        finish(served_at, served_at + served, white_own)
        finish(starts[0], tile_cols, white_own)
        early_sends()
        relay_sends()
        white_far_mid.wait_recv()
        finish(theirs_at, theirs_at + served, white_in)
        for flow in [white_far_end, white_far_mid, white_end] + white_end_both:
            flow.wait_send()

    @pl.when(is_end)
    def _():
        back_edge.wait_recv()
        beside()
        for part in range(PARTS):
            near_part(part)
        early_sends()
        white_end.wait_recv()
        finish(served_at, served_at + served, white_in)
        for k in range(chunks - 1):
            white_end_both[k].wait_recv()
            finish(starts[k], starts[k + 1], white_in)
        white_far_end.wait_recv()
        finish(theirs_at, theirs_at + served, white_in)
        white_end_both[chunks - 1].wait_recv()
        finish(starts[chunks - 1], starts[chunks], white_in)


def put_out(src, dst, sem):
    pieces = sem.shape[0]
    size = src.shape[0] // pieces
    copies = [
        pltpu.make_async_copy(src.at[pl.ds(k * size, size)], dst.at[pl.ds(k * size, size)], sem.at[k])
        for k in range(pieces)
    ]
    for copy in copies:
        copy.start()
    for copy in copies:
        copy.wait()


def pair_on_device(convergence, block_level, near_codes, far_rows, near_factor, far_factor):
    tile_rows, tile_cols, samples, pixels = convergence.shape
    n_rows, n_cols = lax.axis_size("rows"), lax.axis_size("cols")
    near_slots, far_slots = near_codes.shape[2], far_rows.shape[2]
    half = samples // 2
    served = tile_cols // 4
    starts = group_starts(tile_cols, served)
    sizes = [starts[k + 1] - starts[k] for k in range(len(starts) - 1)]
    near_codes = jnp.transpose(near_codes, (0, 2, 1))
    far_codes = jnp.transpose(far_rows, (0, 2, 1))
    dims = (n_rows, n_cols, tile_rows, tile_cols, half, pixels, near_slots, far_slots, served)
    block = (half, pixels)
    bf16, f32, i32 = jnp.bfloat16, jnp.float32, jnp.int32
    all_rows = tile_rows * tile_cols * half
    group_rows = tile_rows * half * max([n_rows * served] + [2 * size for size in sizes])
    dma = pltpu.SemaphoreType.DMA
    scratch = [pltpu.VMEM((n_rows * tile_rows, size) + block, bf16) for size in sizes]
    scratch += [
        pltpu.VMEM((n_rows * tile_rows, served) + block, bf16),
        pltpu.VMEM((tile_rows + 4, tile_cols + 4) + block, bf16),
        pltpu.VMEM((tile_rows, served) + block, bf16),
        pltpu.VMEM((4, 2, 2) + block, bf16),
        pltpu.VMEM((2,) + near_factor.shape, bf16),
        pltpu.VMEM((2,) + far_factor.shape, bf16),
        pltpu.VMEM((2,) + near_codes.shape, i32),
        pltpu.VMEM((n_rows, 2) + far_codes.shape, i32),
        pltpu.SMEM((2,) + near_codes.shape, i32),
        pltpu.SMEM((n_rows, 2) + far_codes.shape, i32),
        pltpu.SMEM(block_level.shape, i32),
        pltpu.VMEM((all_rows, 2 * near_slots // PARTS * pixels), bf16),
        pltpu.VMEM((group_rows, 2 * far_slots * pixels), bf16),
        pltpu.VMEM((all_rows, pixels), f32),
        pltpu.VMEM((group_rows, pixels), f32),
        pltpu.VMEM((3, tile_rows, served) + block, bf16),
        pltpu.VMEM((tile_rows, tile_cols - 2 * served) + block, bf16),
        pltpu.VMEM((tile_rows, tile_cols) + block, bf16),
        pltpu.VMEM((tile_rows, tile_cols) + block, bf16),
        dma((30 + 4 * len(sizes),)),
        dma((30 + 4 * len(sizes),)),
        dma((16 + 3 * len(sizes),)),
    ]
    anywhere = pl.BlockSpec(memory_space=pl.ANY)
    vmem = pl.BlockSpec(memory_space=pltpu.VMEM)
    white = pl.pallas_call(
        functools.partial(pair_kernel, dims),
        out_shape=pltpu.VMEM((tile_rows, tile_cols) + block, bf16),
        in_specs=[anywhere] * 6,
        out_specs=vmem,
        scratch_shapes=scratch,
        compiler_params=pltpu.CompilerParams(
            collective_id=0, has_side_effects=True, vmem_limit_bytes=56 * 1024 * 1024),
    )(convergence, near_codes, far_codes, block_level, near_factor, far_factor)
    return pl.pallas_call(
        put_out,
        out_shape=jax.ShapeDtypeStruct(white.shape, bf16),
        in_specs=[vmem],
        out_specs=anywhere,
        scratch_shapes=[dma((tile_rows,))],
    )(pltpu.with_memory_space_constraint(white, pltpu.VMEM))


def solution(mesh):
    placed = (
        P(("fields", "rows"), "cols", None, None),
        P(("fields", "rows"), "cols"),
        P(("fields", "rows"), "cols", "sub"),
        P(("fields", "rows"), "cols", "sub"),
        P(None, "sub"),
        P(None, "sub"),
    )
    two_middle_tiles = mesh.shape["rows"] - 2 == 2
    return jax.shard_map(
        pair_on_device if two_middle_tiles else on_device,
        mesh=mesh,
        in_specs=placed,
        out_specs=P(("fields", "rows"), "cols", "sub", None),
        check_vma=False,
    )
```
